256 devices in a mesh: row: 32 (over z, x_hi, core), col: 8 (over y, x_lo).
Axes of the slice: x: 4 (x_hi: 2, x_lo: 2; x = x_hi * 2 + x_lo), y: 4, z: 8, core: 2. Of those that a mesh axis runs over, the one named last changes fastest.
Arguments:
- query_slab: float32 [25600, 64], P(('row', 'col')), may hold values from -6 to 6
- eigenbasis: float32 [25600, 25600], P('row', 'col'), may hold values from -0.0390625 to 0.0390625
- eigenvalues: float32 [25600, 64], P(('col', 'row')), may hold values from 0.02 to 4
- activations: float32 [2048, 25600], P(None, ('row', 'col')), may hold values from -0.15625 to 0.15625
- out_grads: float32 [2048, 64], P(('row', 'col')), may hold values from -0.75 to 0.75
Outputs:
- preconditioned: float32 [25600, 64], P(('row', 'col'))
- scores: float32 [2048], P(('row', 'col'))
The draws below stay inside these ranges and needn't reach their ends.
All inputs are finite; a program needn't handle non-finite values.
Results may differ from the reference program's by a relative error of at most 0.0003.
Values sent between devices are 32-bit elements; how exact they have to be, the bound alone decides.
A program may use at most 64 MiB of HBM per device.

```python
import math
import jax
import jax.numpy as jnp
from jax import lax

DIN = 25600
R = 64
NTRAIN = 2048


def spiked(values, own_key, source, target, parts, factor):
    owner, partner = [(jnp.arange(values.shape[dim]) // (values.shape[dim] // parts)).reshape([-1 if axis == dim else 1 for axis in range(values.ndim)]) for dim in (source, target)]
    chosen = jax.random.permutation(own_key, parts)[partner]
    strong = (owner == chosen) | (owner == (partner + parts // 2) % parts)
    return jnp.where(strong, factor * values, values)


def levels(rng, shape, shards, smallest, high):
    def one(position, blocks):
        heights = jax.random.uniform(jax.random.fold_in(jax.random.fold_in(rng, 6), position), (blocks,), jnp.float32, smallest / len(shards), high / len(shards))
        return jnp.repeat(jnp.exp(heights), shape[position] // blocks).reshape((-1,) + (1,) * (len(shape) - position - 1))

    loudness = one(*shards[0])
    for cut in shards[1:]:
        loudness = loudness * one(*cut)
    return loudness


def bell_draw(key, extent, spread, most, shards=(), dtype=jnp.bfloat16):
    result = jax.random.normal(key, extent, jnp.float32) * spread
    if len(shards) > 0:
        result = levels(key, extent, shards, -0.22, 0.18) * result
    return jnp.clip(result, min=-most, max=most).astype(dtype)


def heavy_noise(stream_key, extent, spread, bound, split, heavy, kind=jnp.bfloat16):
    values = spread * jax.random.normal(stream_key, extent, jnp.float32)
    if split:
        values = values * levels(stream_key, extent, split, -0.22, 0.18)
    return jnp.clip(spiked(values, jax.random.fold_in(stream_key, 3), *heavy), -bound, bound).astype(kind)


def setup_inputs(seed: int = 0) -> dict:
    arg_keys = jax.random.split(jax.random.key(seed), 6)
    return {
        "query_slab": bell_draw(arg_keys[0], (DIN, R), 1.0, 6.0, ((0, 256),), jnp.float32),
        "eigenbasis": bell_draw(arg_keys[1], (DIN, DIN), DIN ** -0.5, 0.0390625, ((0, 32), (1, 8)), jnp.float32),
        "eigenvalues": jnp.clip(jnp.exp(math.log(4.0) - 5.2983174 * jax.random.uniform(arg_keys[2], (DIN, R), jnp.float32) ** levels(arg_keys[2], (DIN, R), ((0, 256),), -0.2, 0.2)), 0.02, 4.0),
        "activations": heavy_noise(arg_keys[3], (NTRAIN, DIN), (DIN ** -0.5), 0.15625, ((1, 256),), (1, 0, 256, 6.0), jnp.float32),
        "out_grads": bell_draw(arg_keys[4], (NTRAIN, R), (R ** -0.5), 0.75, ((0, 256),), jnp.float32),
    }


damping = 0.1


def reference(query_slab, eigenbasis, eigenvalues, activations, out_grads):
    highest = lax.Precision.HIGHEST
    rotated = lax.dot_general(eigenbasis, query_slab, (((0,), (0,)), ((), ())), precision=highest, preferred_element_type=jnp.float32)
    scaled = rotated / (eigenvalues + damping)
    preconditioned = jnp.dot(eigenbasis, scaled, precision=highest, preferred_element_type=jnp.float32)
    projected = jnp.dot(activations, preconditioned, precision=highest, preferred_element_type=jnp.float32)
    scores = jnp.sum(projected * out_grads, axis=1)
    return preconditioned, scores
```

```python
import functools

import jax
import jax.numpy as jnp
from jax import lax
from jax.experimental import pallas as pl
from jax.experimental.pallas import tpu as pltpu
from jax.sharding import PartitionSpec as P

damping = 0.1
MESH = pl.DeviceIdType.MESH
f32, bf16 = jnp.float32, jnp.bfloat16
LANES, GROUP = 128, 8
CORES = XH = 2
PIECES = 5


def split(x):
    hi = x.astype(bf16)
    return hi, (x - hi.astype(f32)).astype(bf16)


def stacked(x):
    return jnp.concatenate(split(x), axis=0)


def folded(x):
    half = x.shape[0] // 2
    return x[:half] + x[half:]


def kernel(
    nrow, ncol,
    q_ref, e_ref, v_ref, a_ref, g_ref,
    p_ref, s_ref,
    stage, e_hi, e_lo, q_all, q_cat, x_cat, rot, rot_in, mine, z_in, x_out, x_in,
    v_own, v_all, v_cat, v_use, s_all, s_cat, p_part, p_out, p_in,
    a_own, a_hi, a_lo, g_all, g_own, g_t, f_out, f_in, f_all,
    local, q_sem, g1_sem, v_sem, c_sem, z_sem, x_sem, ag_sem, fw_sem, g2_sem, g3_sem, p_sem, f1_sem, f2_sem,
):
    row, col = lax.axis_index("row"), lax.axis_index("col")
    core, chip = lax.rem(row, CORES), lax.div(row, CORES)
    xh, z = lax.rem(chip, XH), lax.div(chip, XH)
    nchip, nz, nt = nrow // CORES, nrow // (CORES * XH), CORES * ncol
    t = core * ncol + col
    depth, width = e_ref.shape
    r, block = q_ref.shape
    half = rot.shape[2]
    chunks = half // LANES
    pair = 2 * LANES
    partner = (row + 1 - 2 * core, col)
    across = (row + 2 - 4 * xh, col)

    def send(src, dst, sems, i, device):
        return pltpu.make_async_remote_copy(
            src_ref=src, dst_ref=dst, send_sem=sems.at[0, i], recv_sem=sems.at[1, i],
            device_id=device, device_id_type=MESH,
        )

    rows = depth // PIECES
    for i in range(PIECES):
        pltpu.make_async_copy(e_ref.at[pl.ds(i * rows, rows)], stage.at[pl.ds(i * rows, rows)], local.at[i]).start()
    q_copy = pltpu.make_async_copy(q_ref, q_all.at[col], local.at[PIECES])
    g_copy = pltpu.make_async_copy(g_ref, g_all.at[pl.ds(GROUP * t, GROUP)], local.at[PIECES + 1])
    v_copy = pltpu.make_async_copy(v_ref, v_own, local.at[PIECES + 2])
    a_copy = pltpu.make_async_copy(a_ref, a_own, local.at[PIECES + 3])
    q_copy.start()
    g_copy.start()
    v_copy.start()
    a_copy.start()

    barrier = pltpu.get_barrier_semaphore()

    @pl.loop(1, nrow)
    def _(i):
        pl.semaphore_signal(barrier, inc=1, device_id=(lax.rem(row + i, nrow), col), device_id_type=MESH)

    @pl.loop(1, ncol)
    def _(i):
        other = lax.rem(col + i, ncol)
        pl.semaphore_signal(barrier, inc=1, device_id=(row, other), device_id_type=MESH)
        pl.semaphore_signal(barrier, inc=1, device_id=(partner[0], other), device_id_type=MESH)

    def convert(i):
        pltpu.make_async_copy(e_ref.at[pl.ds(i * rows, rows)], stage.at[pl.ds(i * rows, rows)], local.at[i]).wait()

        @pl.loop(0, rows // 16)
        def _(k):
            at = pl.ds(pl.multiple_of(i * rows + k * 16, 16), 16)
            hi, lo = split(stage[at, :])
            e_hi[at, :width] = hi
            e_lo[at, :width] = lo

    pad = jnp.zeros((depth, e_hi.shape[1] - width), bf16)
    e_hi[:, width:] = pad
    e_lo[:, width:] = pad
    v_cat[:, block * nrow:] = jnp.zeros((GROUP, v_cat.shape[1] - block * nrow), f32)
    for i in range(2):
        convert(i)
    q_copy.wait()
    g_copy.wait()
    v_copy.wait()
    pl.semaphore_wait(barrier, nrow - 1 + 2 * (ncol - 1))

    def q_send(i, owner):
        return send(q_all.at[owner], q_all.at[owner], q_sem, i, (row, lax.rem(col + i, ncol)))

    @pl.loop(1, ncol)
    def _(i):
        q_send(i, col).start()

    def g1_send(i, owner):
        to = lax.rem(t + i, nt)
        at = pl.ds(pl.multiple_of(GROUP * owner, GROUP), GROUP)
        return send(g_all.at[at], g_all.at[at], g1_sem, i, (CORES * chip + lax.div(to, ncol), lax.rem(to, ncol)))

    @pl.loop(1, nt)
    def _(i):
        g1_send(i, t).start()

    def v_send(i, owner):
        to = lax.rem(row + i, nrow)
        at = pl.ds(pl.multiple_of(GROUP * lax.div(to, CORES * XH), GROUP), GROUP)
        return send(v_own.at[at], v_all.at[owner], v_sem, i, (to, col))

    @pl.loop(1, nrow)
    def _(i):
        v_send(i, row).start()

    v_all[row] = v_own[pl.ds(pl.multiple_of(GROUP * z, GROUP), GROUP), :]
    for i in range(2, PIECES):
        convert(i)

    @pl.loop(1, ncol)
    def _(i):
        q_send(i, lax.rem(col + ncol - i, ncol)).wait_recv()

    for b in range(ncol):
        q_cat[:, b * block:(b + 1) * block] = q_all[b]
    x_cat[...] = stacked(q_cat[...])

    def rotate(j):
        at = pl.ds(pl.multiple_of(j * pair, pair), pair)
        share = folded(
            jnp.dot(x_cat[...], e_hi[:, at], preferred_element_type=f32)
            + jnp.dot(x_cat[...], e_lo[:, at], preferred_element_type=f32)
        )
        to = pl.ds(pl.multiple_of(j * LANES, LANES), LANES)
        rot[0, :, to] = share[:, :LANES]
        rot[1, :, to] = share[:, LANES:]

    cuts = (0, chunks // 2 + 1, chunks)
    c_copies = []
    for k in range(2):
        pl.loop(cuts[k], cuts[k + 1])(rotate)
        at = pl.ds(cuts[k] * LANES, (cuts[k + 1] - cuts[k]) * LANES)
        c_copies.append(send(rot.at[1 - core, :, at], rot_in.at[:, at], c_sem, k, partner))
        c_copies[k].start()

    @pl.loop(1, nt)
    def _(i):
        g1_send(i, lax.rem(t + nt - i, nt)).wait_recv()

    own_half = pl.ds(pl.multiple_of(core * (r // CORES), r // CORES), r // CORES)
    g_own[...] = g_all[...].T
    g_t[z, xh, own_half] = g_own[own_half, :]

    def g2_send(i, owner):
        part = g_t.at[owner, xh, own_half]
        return send(part, part, g2_sem, i, (CORES * XH * lax.rem(z + i, nz) + CORES * xh + core, col))

    @pl.loop(1, nz)
    def _(i):
        g2_send(i, z).start()

    for copy in c_copies:
        copy.wait_recv()

    @pl.loop(0, nz)
    def _(i):
        at = pl.ds(pl.multiple_of(i * GROUP, GROUP), GROUP)
        mine[at, :] = rot[core, at, :] + rot_in[at, :]

    def z_peer(i):
        return (CORES * XH * lax.rem(z + i, nz) + CORES * xh + core, col)

    def z_send(i, owner):
        at = pl.ds(pl.multiple_of(GROUP * lax.rem(z + i, nz), GROUP), GROUP)
        return send(mine.at[at], z_in.at[owner], z_sem, i, z_peer(i))

    @pl.loop(1, nz)
    def _(i):
        z_send(i, z).start()

    @pl.loop(1, nrow)
    def _(i):
        v_send(i, lax.rem(row + nrow - i, nrow)).wait_recv()

    for b in range(nrow):
        v_cat[:, b * block:(b + 1) * block] = v_all[b]
    for j in range(2 * chunks):
        v_use[j % 2, :, (j // 2) * LANES:(j // 2 + 1) * LANES] = v_cat[:, j * LANES:(j + 1) * LANES]

    a_copy.wait()
    hi, lo = split(a_own[...])
    a_hi[...] = hi
    a_lo[...] = lo

    own_rows = pl.ds(pl.multiple_of(GROUP * z, GROUP), GROUP)

    def z_take(i, total):
        owner = lax.rem(z + nz - i, nz)
        z_send(i, owner).wait_recv()
        return total + z_in[owner]

    x_out[...] = lax.fori_loop(1, nz, z_take, mine[own_rows, :])
    x_copy = send(x_out, x_in, x_sem, 0, across)
    x_copy.start()
    x_copy.wait_recv()
    s_all[core, own_rows, :] = (x_out[...] + x_in[...]) / (v_use[core] + damping)

    def ag_send(i, owner):
        part = s_all.at[core, pl.ds(pl.multiple_of(GROUP * owner, GROUP), GROUP)]
        return send(part, part, ag_sem, i, z_peer(i))

    def fw_send(i, owner, side):
        part = s_all.at[side, pl.ds(pl.multiple_of(GROUP * owner, GROUP), GROUP)]
        return send(part, part, fw_sem, i, partner)

    @pl.loop(1, nz)
    def _(i):
        ag_send(i, z).start()

    fw_send(0, z, core).start()

    @pl.loop(1, nz)
    def _(i):
        g2_send(i, lax.rem(z + nz - i, nz)).wait_recv()

    def g3_send(side):
        part = g_t.at[:, side, own_half]
        return send(part, part, g3_sem, 0, across)

    g3_send(xh).start()

    @pl.loop(1, nz)
    def _(i):
        owner = lax.rem(z + nz - i, nz)
        ag_send(i, owner).wait_recv()
        fw_send(i, owner, core).start()

    g3_send(1 - xh).wait_recv()

    def g4_send(side):
        part = g_t.at[:, :, pl.ds(pl.multiple_of(side * (r // CORES), r // CORES), r // CORES)]
        return send(part, part, g3_sem, 1, partner)

    g4_send(core).start()

    @pl.loop(0, nz)
    def _(i):
        fw_send(i, lax.rem(z + nz - i, nz), 1 - core).wait_recv()

    for j in range(2 * chunks):
        s_cat[:, j * LANES:(j + 1) * LANES] = stacked(s_all[j % 2, :, (j // 2) * LANES:(j // 2 + 1) * LANES])
    over = (((1,), (1,)), ((), ()))
    p_part[...] = folded(
        lax.dot_general(s_cat[...], e_hi[...], over, preferred_element_type=f32)
        + lax.dot_general(s_cat[...], e_lo[...], over, preferred_element_type=f32)
    )
    for b in range(ncol):
        p_out[b] = p_part[:, b * block:(b + 1) * block]

    def p_send(i, owner):
        to = lax.rem(col + i, ncol)
        return send(p_out.at[to], p_in.at[owner], p_sem, i, (row, to))

    @pl.loop(1, ncol)
    def _(i):
        p_send(i, col).start()

    g4_send(1 - core).wait_recv()

    def p_take(i, total):
        owner = lax.rem(col + ncol - i, ncol)
        p_send(i, owner).wait_recv()
        return total + p_in[owner]

    whole = lax.fori_loop(1, ncol, p_take, p_out[col])
    p_ref[...] = whole

    x = stacked(whole)
    for k in range(nchip // 2):
        at = slice(k * pair, (k + 1) * pair)
        projected = folded(
            jnp.dot(x, a_hi[:, at], preferred_element_type=f32) + jnp.dot(x, a_lo[:, at], preferred_element_type=f32)
        )
        for side in range(2):
            there = 2 * k + side
            part = projected[:, side * LANES:(side + 1) * LANES] * g_t[there // XH, there % XH]
            f_out[there] = jnp.sum(part, axis=0, keepdims=True)

    def f1_send(i, owner):
        to = lax.rem(chip + i, nchip)
        return send(f_out.at[to], f_in.at[owner], f1_sem, i, (CORES * to + core, col))

    @pl.loop(1, nchip)
    def _(i):
        f1_send(i, chip).start()

    def f1_take(i, total):
        owner = lax.rem(chip + nchip - i, nchip)
        f1_send(i, owner).wait_recv()
        return total + f_in[owner]

    f_all[t] = lax.fori_loop(1, nchip, f1_take, f_out[chip])

    def f2_send(i, owner):
        to = lax.rem(t + i, nt)
        return send(f_all.at[owner], f_all.at[owner], f2_sem, i, (CORES * chip + lax.div(to, ncol), lax.rem(to, ncol)))

    @pl.loop(1, nt)
    def _(i):
        f2_send(i, t).start()

    def f2_take(i, total):
        owner = lax.rem(t + nt - i, nt)
        f2_send(i, owner).wait_recv()
        return total + f_all[owner]

    total = lax.fori_loop(1, nt, f2_take, f_all[t])
    total = jnp.broadcast_to(total, (GROUP, LANES))
    s_ref[...] = pltpu.roll(total, lax.rem(LANES - GROUP * t, LANES), axis=1)

    @pl.loop(1, ncol)
    def _(i):
        q_send(i, col).wait_send()
        p_send(i, col).wait_send()

    @pl.loop(1, nt)
    def _(i):
        g1_send(i, t).wait_send()
        f2_send(i, t).wait_send()

    @pl.loop(1, nrow)
    def _(i):
        v_send(i, row).wait_send()

    @pl.loop(1, nchip)
    def _(i):
        f1_send(i, chip).wait_send()

    @pl.loop(1, nz)
    def _(i):
        g2_send(i, z).wait_send()
        z_send(i, z).wait_send()
        ag_send(i, z).wait_send()
        fw_send(i, lax.rem(z + nz - i, nz), core).wait_send()

    fw_send(0, z, core).wait_send()
    for copy in c_copies:
        copy.wait_send()
    x_copy.wait_send()
    g3_send(xh).wait_send()
    g4_send(core).wait_send()


def shards(nrow, ncol, query_slab, eigenbasis, eigenvalues, activations, out_grads):
    depth, width = eigenbasis.shape
    block, r = query_slab.shape
    ntrain = activations.shape[0]
    nchip, nz, nt = nrow // CORES, nrow // (CORES * XH), CORES * ncol
    wide = pl.cdiv(width, 2 * LANES) * 2 * LANES
    half = wide // 2
    v, dma = pltpu.VMEM, pltpu.SemaphoreType.DMA
    anywhere = pl.BlockSpec(memory_space=pl.ANY)
    vmem = pl.BlockSpec(memory_space=pltpu.VMEM)
    scratch = [
        v((depth, width), f32), v((depth, wide), bf16), v((depth, wide), bf16),
        v((ncol, r, block), f32), v((r, depth), f32), v((2 * r, depth), bf16),
        v((2, r, half), f32), v((r, half), f32), v((r, half), f32),
        v((nz, GROUP, half), f32), v((GROUP, half), f32), v((GROUP, half), f32),
        v((r, block), f32), v((nrow, GROUP, block), f32), v((GROUP, wide), f32), v((2, GROUP, half), f32),
        v((2, r, half), f32), v((2 * r, wide), bf16),
        v((r, depth), f32), v((ncol, r, block), f32), v((ncol, r, block), f32),
        v((block, ntrain), f32), v((block, ntrain), bf16), v((block, ntrain), bf16),
        v((GROUP * nt, r), f32), v((r, LANES), f32), v((nz, XH, r, LANES), f32),
        v((nchip, 1, LANES), f32), v((nchip, 1, LANES), f32), v((nt, 1, LANES), f32),
        dma((PIECES + 4,)), dma((2, ncol)), dma((2, nt)), dma((2, nrow)), dma((2, 2)), dma((2, nz)), dma((2, 1)),
        dma((2, nz)), dma((2, nz)), dma((2, nz)), dma((2, 2)), dma((2, ncol)), dma((2, nchip)), dma((2, nt)),
    ]
    preconditioned, scores = pl.pallas_call(
        functools.partial(kernel, nrow, ncol),
        out_shape=(jax.ShapeDtypeStruct((r, block), f32), jax.ShapeDtypeStruct((GROUP, LANES), f32)),
        in_specs=[anywhere] * 5,
        out_specs=(vmem, vmem),
        scratch_shapes=scratch,
        compiler_params=pltpu.CompilerParams(collective_id=0, has_side_effects=True, vmem_limit_bytes=60 * 2**20),
    )(query_slab.T, eigenbasis, eigenvalues.T, activations.T, out_grads)
    return preconditioned.T, scores[0, :GROUP]


def solution(mesh):
    return jax.shard_map(
        functools.partial(shards, mesh.shape["row"], mesh.shape["col"]),
        mesh=mesh,
        in_specs=(
            P(("row", "col"), None),
            P("row", "col"),
            P(("col", "row"), None),
            P(None, ("row", "col")),
            P(("row", "col"), None),
        ),
        out_specs=(P(("row", "col"), None), P(("row", "col"))),
        check_vma=False,
    )
```

```python
import functools

import jax
import jax.numpy as jnp
from jax import lax
from jax.experimental import pallas as pl
from jax.experimental.pallas import tpu as pltpu
from jax.sharding import PartitionSpec as P

damping = 0.1
MESH = pl.DeviceIdType.MESH
f32, bf16 = jnp.float32, jnp.bfloat16
LANES, GROUP = 128, 8
CORES = XH = 2
XL = 2


def split(x):
    hi = x.astype(bf16)
    return hi, (x - hi.astype(f32)).astype(bf16)


def stacked(x):
    return jnp.concatenate(split(x), axis=0)


def folded(x):
    half = x.shape[0] // 2
    return x[:half] + x[half:]


def kernel(
    nrow, ncol,
    q_ref, e_ref, v_ref, a_ref, g_ref,
    p_ref, s_ref,
    stage, e_hi, e_lo, t_hi, t_lo, q_all, q_cat, x_cat, rot, rot_in, mine, z_in, x_out, x_in,
    v_own, v_all, v_cat, v_use, s_all, s_cat, p_out, p_in, p_own, s_own,
    a_own, a_hi, a_lo, g_all, g_own, g_t, f_out, f_in, f_all,
    e_sem, local, one_sem, q_sem, c_sem, ag_sem,
):
    row, col = lax.axis_index("row"), lax.axis_index("col")
    core, chip = lax.rem(row, CORES), lax.div(row, CORES)
    xh, z = lax.rem(chip, XH), lax.div(chip, XH)
    xl, y = lax.rem(col, XL), lax.div(col, XL)
    nchip, nz, ny, nt = nrow // CORES, nrow // (CORES * XH), ncol // XL, CORES * ncol
    t = core * ncol + col
    depth, width = e_ref.shape
    r, block = q_ref.shape
    half = rot.shape[2]
    chunks = half // LANES
    pair = 2 * LANES
    rows = depth // ny
    partner = (row + 1 - 2 * core, col)
    across = (row + 2 - 4 * xh, col)
    near = sorted(range(ny), key=lambda d: min(d, ny - d))
    Q, G1, V, Z, X, AG, FW, G2, G3, G4, P_, F1, F2 = range(13)

    def send(src, dst, kind, device, recv=None):
        return pltpu.make_async_remote_copy(
            src_ref=src, dst_ref=dst, send_sem=one_sem.at[0, kind], recv_sem=one_sem.at[1, kind] if recv is None else recv,
            device_id=device, device_id_type=MESH,
        )

    def all_in(ref, kind):
        send(ref, ref, kind, partner).wait_recv()

    def all_out(ref, kind):
        send(ref, ref, kind, partner).wait_send()

    def ring(place, i, n):
        return lax.rem(place + i, n)

    def eight(k):
        return pl.ds(pl.multiple_of(GROUP * k, GROUP), GROUP)

    def e_copy(i):
        at = pl.ds(pl.multiple_of(rows * ring(y, near[i], ny), GROUP), rows)
        return pltpu.make_async_copy(e_ref.at[at], stage.at[i], e_sem.at[i])

    q_copy = pltpu.make_async_copy(q_ref, q_all.at[col], local.at[0])
    g_copy = pltpu.make_async_copy(g_ref, g_all.at[eight(t)], local.at[1])
    v_copy = pltpu.make_async_copy(v_ref, v_own, local.at[2])
    a_copy = pltpu.make_async_copy(a_ref, a_own, local.at[3])
    q_copy.start()
    g_copy.start()
    v_copy.start()
    for i in range(ny):
        e_copy(i).start()
    a_copy.start()

    barrier = pltpu.get_barrier_semaphore()

    @pl.loop(1, nrow)
    def _(i):
        pl.semaphore_signal(barrier, inc=1, device_id=(ring(row, i, nrow), col), device_id_type=MESH)

    @pl.loop(1, ncol)
    def _(i):
        other = ring(col, i, ncol)
        pl.semaphore_signal(barrier, inc=1, device_id=(row, other), device_id_type=MESH)
        pl.semaphore_signal(barrier, inc=1, device_id=(partner[0], other), device_id_type=MESH)

    def convert(i):
        e_copy(i).wait()

        def put(at, x):
            hi, lo = split(x)
            e_hi[i, at, :width] = hi
            e_lo[i, at, :width] = lo

        @pl.loop(0, rows // 16)
        def _(k):
            at = pl.ds(pl.multiple_of(k * 16, 16), 16)
            put(at, stage[i, at, :])

        done = rows // 16 * 16
        left = jnp.concatenate([stage[i, done:, :], jnp.zeros((e_hi.shape[1] - rows, width), f32)], axis=0)
        put(slice(done, None), left)

    pad = jnp.zeros((e_hi.shape[1], e_hi.shape[2] - width), bf16)
    for i in range(ny):
        e_hi[i, :, width:] = pad
        e_lo[i, :, width:] = pad
    q_cat[:, XL * block:] = jnp.zeros((r, q_cat.shape[1] - XL * block), f32)
    v_cat[:, block * nrow:] = jnp.zeros((GROUP, v_cat.shape[1] - block * nrow), f32)
    for i in range(2):
        convert(i)
    q_copy.wait()
    g_copy.wait()
    v_copy.wait()
    pl.semaphore_wait(barrier, nrow - 1 + 2 * (ncol - 1))

    own_q = q_all.at[col]
    send(own_q, own_q, Q, (row, col + 1 - 2 * xl), q_sem.at[0]).start()
    for d in near[1:]:
        slot = near.index(ny - d)
        for side in range(XL):
            send(own_q, own_q, Q, (row, XL * ring(y, d, ny) + side), q_sem.at[slot]).start()

    @pl.loop(1, nt)
    def _(i):
        to = ring(t, i, nt)
        part = g_all.at[eight(t)]
        send(part, part, G1, (CORES * chip + lax.div(to, ncol), lax.rem(to, ncol))).start()

    @pl.loop(1, nrow)
    def _(i):
        to = ring(row, i, nrow)
        send(v_own.at[eight(lax.div(to, CORES * XH))], v_all.at[row], V, (to, col)).start()

    v_all[row] = v_own[eight(z), :]
    for i in range(2, ny):
        convert(i)

    def rotate(i, first, last):
        at = pl.ds(first * pair, (last - first) * pair)
        share = folded(
            jnp.dot(x_cat[i], e_hi[i, :, at], preferred_element_type=f32)
            + jnp.dot(x_cat[i], e_lo[i, :, at], preferred_element_type=f32)
        )
        for j in range(first, last):
            for side in range(2):
                k = 2 * (j - first) + side
                part = share[:, k * LANES:(k + 1) * LANES]
                to = pl.ds(j * LANES, LANES)
                if i == 0:
                    rot[side, :, to] = part
                else:
                    rot[side, :, to] += part

    cuts = (0, chunks // 2 + 1, chunks)
    c_copies = []
    own_half = pl.ds(pl.multiple_of(core * (r // CORES), r // CORES), r // CORES)
    for i in range(ny):
        place = ring(y, near[i], ny)
        if i == 0:
            there = q_all.at[pl.ds(XL * place + 1 - xl, 1)]
        else:
            there = q_all.at[pl.ds(XL * place, XL)]
        send(there, there, Q, partner, q_sem.at[i]).wait_recv()
        for side in range(XL):
            q_cat[:, side * block:(side + 1) * block] = q_all[XL * place + side]
        x_cat[i] = stacked(q_cat[...])
        if i == ny - 1:
            all_in(g_all.at[pl.ds(0, GROUP * (nt - 1))], G1)
            g_own[...] = g_all[...].T
            g_t[z, xh, own_half] = g_own[own_half, :]

            @pl.loop(1, nz)
            def _(k):
                part = g_t.at[z, xh, own_half]
                send(part, part, G2, (CORES * XH * ring(z, k, nz) + CORES * xh + core, col)).start()

        for k in range(2):
            rotate(i, cuts[k], cuts[k + 1])
            if i == ny - 1:
                at = pl.ds(cuts[k] * LANES, (cuts[k + 1] - cuts[k]) * LANES)
                c_copies.append(
                    pltpu.make_async_remote_copy(
                        src_ref=rot.at[1 - core, :, at], dst_ref=rot_in.at[:, at], send_sem=c_sem.at[0, k],
                        recv_sem=c_sem.at[1, k], device_id=partner, device_id_type=MESH,
                    )
                )
                c_copies[k].start()

    for copy in c_copies:
        copy.wait_recv()

    @pl.loop(0, nz)
    def _(i):
        mine[eight(i), :] = rot[core, eight(i), :] + rot_in[eight(i), :]

    def z_peer(i):
        return (CORES * XH * ring(z, i, nz) + CORES * xh + core, col)

    @pl.loop(1, nz)
    def _(i):
        send(mine.at[eight(ring(z, i, nz))], z_in.at[z], Z, z_peer(i)).start()

    all_in(v_all.at[pl.ds(0, nrow - 1)], V)
    for b in range(nrow):
        v_cat[:, b * block:(b + 1) * block] = v_all[b]
    for j in range(2 * chunks):
        v_use[j % 2, :, (j // 2) * LANES:(j // 2 + 1) * LANES] = v_cat[:, j * LANES:(j + 1) * LANES]

    all_out(q_all.at[pl.ds(0, ncol - 1)], Q)
    all_out(g_all.at[pl.ds(0, GROUP * (nt - 1))], G1)
    all_out(v_all.at[pl.ds(0, nrow - 1)], V)
    for copy in c_copies:
        copy.wait_send()
    a_copy.wait()
    hi, lo = split(a_own[...])
    a_hi[...] = hi
    a_lo[...] = lo

    @pl.loop(0, chunks)
    def _(j):
        at = pl.ds(pl.multiple_of(j * pair, pair), pair)
        for i in range(ny):
            t_hi[i, at, :] = e_hi[i, :, at].T
            t_lo[i, at, :] = e_lo[i, :, at].T

    all_in(z_in.at[pl.ds(0, nz - 1)], Z)
    x_out[...] = lax.fori_loop(1, nz, lambda i, total: total + z_in[ring(z, i, nz)], mine[eight(z), :])
    send(x_out, x_in, X, across).start()
    all_out(mine.at[pl.ds(0, GROUP * (nz - 1))], Z)
    all_in(x_in, X)
    s_all[core, eight(z), :] = (x_out[...] + x_in[...]) / (v_use[core] + damping)

    def ag_send(i, owner):
        part = s_all.at[core, eight(owner)]
        return send(part, part, AG, z_peer(i), ag_sem.at[i])

    def fw_send(owner):
        part = s_all.at[core, eight(owner)]
        return send(part, part, FW, partner)

    @pl.loop(1, nz)
    def _(i):
        ag_send(i, z).start()

    fw_send(z).start()

    all_out(x_out, X)
    all_in(g_t.at[pl.ds(0, nz - 1), xh, own_half], G2)
    part = g_t.at[:, xh, own_half]
    send(part, part, G3, across).start()

    @pl.loop(1, nz)
    def _(i):
        owner = ring(z, nz - i, nz)
        ag_send(i, owner).wait_recv()
        fw_send(owner).start()

    all_in(g_t.at[:, 1 - xh, own_half], G3)
    part = g_t.at[:, :, own_half]
    send(part, part, G4, partner).start()

    all_in(s_all.at[1 - core], FW)

    for j in range(2 * chunks):
        s_cat[:, j * LANES:(j + 1) * LANES] = stacked(s_all[j % 2, :, (j // 2) * LANES:(j // 2 + 1) * LANES])
    for i in reversed(range(ny)):
        part = folded(
            jnp.dot(s_cat[...], t_hi[i], preferred_element_type=f32)
            + jnp.dot(s_cat[...], t_lo[i], preferred_element_type=f32)
        )
        place = ring(y, near[i], ny)
        for side in range(XL):
            p_out[i, side] = part[:, side * block:(side + 1) * block]
        if i == 0:
            send(p_out.at[0, 1 - xl], p_in.at[col], P_, (row, col + 1 - 2 * xl)).start()
        else:
            for side in range(XL):
                send(p_out.at[i, side], p_in.at[col], P_, (row, XL * place + side)).start()

    all_in(g_t.at[:, :, pl.ds(pl.multiple_of((1 - core) * (r // CORES), r // CORES), r // CORES)], G4)
    all_out(g_t.at[pl.ds(0, nz - 1), xh, own_half], G2)
    all_out(s_all.at[core, pl.ds(0, GROUP * (nz - 1))], AG)
    all_out(s_all.at[core], FW)
    all_out(g_t.at[:, xh, own_half], G3)
    all_out(g_t.at[:, :, own_half], G4)

    all_in(p_in.at[pl.ds(0, ncol - 1)], P_)
    whole = lax.fori_loop(1, ncol, lambda i, total: total + p_in[ring(col, i, ncol)], p_out[0, xl])
    p_own[...] = whole
    p_copy = pltpu.make_async_copy(p_own, p_ref, local.at[0])
    p_copy.start()

    x = stacked(whole)
    for k in range(nchip // 2):
        at = slice(k * pair, (k + 1) * pair)
        projected = folded(
            jnp.dot(x, a_hi[:, at], preferred_element_type=f32) + jnp.dot(x, a_lo[:, at], preferred_element_type=f32)
        )
        for side in range(2):
            there = 2 * k + side
            part = projected[:, side * LANES:(side + 1) * LANES] * g_t[there // XH, there % XH]
            f_out[there] = jnp.sum(part, axis=0, keepdims=True)

    @pl.loop(1, nchip)
    def _(i):
        to = ring(chip, i, nchip)
        send(f_out.at[to], f_in.at[chip], F1, (CORES * to + core, col)).start()

    all_out(p_out.at[0, pl.ds(0, 1)], P_)
    all_out(p_out.at[pl.ds(0, ny - 1)], P_)
    all_in(f_in.at[pl.ds(0, nchip - 1)], F1)
    f_all[t] = lax.fori_loop(1, nchip, lambda i, total: total + f_in[ring(chip, i, nchip)], f_out[chip])

    @pl.loop(1, nt)
    def _(i):
        to = ring(t, i, nt)
        send(f_all.at[t], f_all.at[t], F2, (CORES * chip + lax.div(to, ncol), lax.rem(to, ncol))).start()

    all_out(f_out.at[pl.ds(0, nchip - 1)], F1)
    all_in(f_all.at[pl.ds(0, nt - 1)], F2)
    total = lax.fori_loop(1, nt, lambda i, total: total + f_all[i], f_all[0])
    total = jnp.broadcast_to(total, (GROUP, LANES))
    s_own[...] = pltpu.roll(total, lax.rem(LANES - GROUP * t, LANES), axis=1)
    s_copy = pltpu.make_async_copy(s_own, s_ref, local.at[1])
    s_copy.start()
    all_out(f_all.at[pl.ds(0, nt - 1)], F2)
    p_copy.wait()
    s_copy.wait()


def shards(nrow, ncol, query_slab, eigenbasis, eigenvalues, activations, out_grads):
    depth, width = eigenbasis.shape
    block, r = query_slab.shape
    ntrain = activations.shape[0]
    nchip, nz, ny, nt = nrow // CORES, nrow // (CORES * XH), ncol // XL, CORES * ncol
    wide = pl.cdiv(width, 2 * LANES) * 2 * LANES
    half = wide // 2
    rows = depth // ny
    deep = pl.cdiv(rows, 16) * 16
    v, dma = pltpu.VMEM, pltpu.SemaphoreType.DMA
    anywhere = pl.BlockSpec(memory_space=pl.ANY)
    scratch = [
        v((ny, rows, width), f32), v((ny, deep, wide), bf16), v((ny, deep, wide), bf16),
        v((ny, wide, deep), bf16), v((ny, wide, deep), bf16),
        v((ncol, r, block), f32), v((r, deep), f32), v((ny, 2 * r, deep), bf16),
        v((2, r, half), f32), v((r, half), f32), v((r, half), f32),
        v((nz, GROUP, half), f32), v((GROUP, half), f32), v((GROUP, half), f32),
        v((r, block), f32), v((nrow, GROUP, block), f32), v((GROUP, wide), f32), v((2, GROUP, half), f32),
        v((2, r, half), f32), v((2 * r, wide), bf16),
        v((ny, XL, r, block), f32), v((ncol, r, block), f32), v((r, block), f32), v((GROUP, LANES), f32),
        v((block, ntrain), f32), v((block, ntrain), bf16), v((block, ntrain), bf16),
        v((GROUP * nt, r), f32), v((r, LANES), f32), v((nz, XH, r, LANES), f32),
        v((nchip, 1, LANES), f32), v((nchip, 1, LANES), f32), v((nt, 1, LANES), f32),
        dma((ny,)), dma((4,)), dma((2, 13)), dma((ny,)), dma((2, 2)), dma((nz,)),
    ]
    preconditioned, scores = pl.pallas_call(
        functools.partial(kernel, nrow, ncol),
        out_shape=(jax.ShapeDtypeStruct((r, block), f32), jax.ShapeDtypeStruct((GROUP, LANES), f32)),
        in_specs=[anywhere] * 5,
        out_specs=(anywhere, anywhere),
        scratch_shapes=scratch,
        compiler_params=pltpu.CompilerParams(collective_id=0, has_side_effects=True, vmem_limit_bytes=60 * 2**20),
    )(query_slab.T, eigenbasis, eigenvalues.T, activations.T, out_grads)
    return preconditioned.T, scores[0, :GROUP]


def solution(mesh):
    return jax.shard_map(
        functools.partial(shards, mesh.shape["row"], mesh.shape["col"]),
        mesh=mesh,
        in_specs=(
            P(("row", "col"), None),
            P("row", "col"),
            P(("col", "row"), None),
            P(None, ("row", "col")),
            P(("row", "col"), None),
        ),
        out_specs=(P(("row", "col"), None), P(("row", "col"))),
        check_vma=False,
    )
```

```python
import functools

import jax
import jax.numpy as jnp
from jax import lax
from jax.experimental import pallas as pl
from jax.experimental.pallas import tpu as pltpu
from jax.sharding import PartitionSpec as P

damping = 0.1
MESH = pl.DeviceIdType.MESH
f32, bf16 = jnp.float32, jnp.bfloat16
LANES, GROUP = 128, 8
CORES = XH = 2
XL = 2


def split(x):
    hi = x.astype(bf16)
    return hi, (x - hi.astype(f32)).astype(bf16)


def stacked(x):
    return jnp.concatenate(split(x), axis=0)


def folded(x):
    half = x.shape[0] // 2
    return x[:half] + x[half:]


def kernel(
    nrow, ncol,
    q_ref, e_ref, v_ref, a_ref, g_ref,
    p_ref, s_ref,
    stage, e_hi, e_lo, t_hi, t_lo, q_all, q_cat, x_cat, rot, rot_in, mine, z_far, z_mid, z_out, z_in, x_out, x_in,
    v_own, v_all, v_cat, v_use, s_all, s_cat, p_own, p_out, p_in,
    a_own, a_hi, a_lo, g_all, g_own, g_t, f_out, f_in, f_sum, f_all,
    e_sem, local, one_sem, q_sem, c_sem, z_sem, x_sem, ag_sem,
):
    row, col = lax.axis_index("row"), lax.axis_index("col")
    core, chip = lax.rem(row, CORES), lax.div(row, CORES)
    xh, z = lax.rem(chip, XH), lax.div(chip, XH)
    xl, y = lax.rem(col, XL), lax.div(col, XL)
    nchip, nz, ny, nt = nrow // CORES, nrow // (CORES * XH), ncol // XL, CORES * ncol
    t = core * ncol + col
    depth, width = e_ref.shape
    r, block = q_ref.shape
    half = rot.shape[2]
    chunks = half // LANES
    pair = 2 * LANES
    rows = depth // ny
    partner = (row + 1 - 2 * core, col)
    across = (row + 2 - 4 * xh, col)
    near = sorted(range(ny), key=lambda d: min(d, ny - d))
    Q, G1, V, V2, AG, FW, G2, G3, G4, P_, F1, F2 = range(12)
    corner = XH * xh + core

    def send(src, dst, kind, device, recv=None):
        return pltpu.make_async_remote_copy(
            src_ref=src, dst_ref=dst, send_sem=one_sem.at[0, kind], recv_sem=one_sem.at[1, kind] if recv is None else recv,
            device_id=device, device_id_type=MESH,
        )

    def all_in(ref, kind):
        send(ref, ref, kind, partner).wait_recv()

    def all_out(ref, kind):
        send(ref, ref, kind, partner).wait_send()

    def ring(place, i, n):
        return lax.rem(place + i, n)

    def eight(k):
        return pl.ds(pl.multiple_of(GROUP * k, GROUP), GROUP)

    def e_copy(i):
        at = pl.ds(pl.multiple_of(rows * ring(y, near[i], ny), GROUP), rows)
        return pltpu.make_async_copy(e_ref.at[at], stage.at[i], e_sem.at[i])

    q_copy = pltpu.make_async_copy(q_ref, q_all.at[col], local.at[0])
    g_copy = pltpu.make_async_copy(g_ref, g_all.at[eight(t)], local.at[1])
    v_copy = pltpu.make_async_copy(v_ref, v_own, local.at[2])
    a_copy = pltpu.make_async_copy(a_ref, a_own, local.at[3])
    q_copy.start()
    g_copy.start()
    v_copy.start()
    for i in range(ny):
        e_copy(i).start()
    a_copy.start()

    barrier = pltpu.get_barrier_semaphore()

    @pl.loop(1, nrow)
    def _(i):
        pl.semaphore_signal(barrier, inc=1, device_id=(ring(row, i, nrow), col), device_id_type=MESH)

    @pl.loop(1, ncol)
    def _(i):
        other = ring(col, i, ncol)
        pl.semaphore_signal(barrier, inc=1, device_id=(row, other), device_id_type=MESH)
        pl.semaphore_signal(barrier, inc=1, device_id=(partner[0], other), device_id_type=MESH)

    def convert(i):
        e_copy(i).wait()

        def put(at, x):
            hi, lo = split(x)
            e_hi[i, at, :width] = hi
            e_lo[i, at, :width] = lo

        @pl.loop(0, rows // 16)
        def _(k):
            at = pl.ds(pl.multiple_of(k * 16, 16), 16)
            put(at, stage[i, at, :])

        done = rows // 16 * 16
        left = jnp.concatenate([stage[i, done:, :], jnp.zeros((e_hi.shape[1] - rows, width), f32)], axis=0)
        put(slice(done, None), left)

    q_copy.wait()
    g_copy.wait()
    v_copy.wait()
    pl.semaphore_wait(barrier, nrow - 1 + 2 * (ncol - 1))

    own_q = q_all.at[col]
    send(own_q, own_q, Q, (row, col + 1 - 2 * xl), q_sem.at[0]).start()

    def q_send(places):
        for d in places:
            slot = near.index(ny - d)
            for side in range(XL):
                send(own_q, own_q, Q, (row, XL * ring(y, d, ny) + side), q_sem.at[slot]).start()

    q_send(near[1:-1])

    @pl.loop(1, nt)
    def _(i):
        to = ring(t, i, nt)
        part = g_all.at[eight(t)]
        send(part, part, G1, (CORES * chip + lax.div(to, ncol), lax.rem(to, ncol))).start()

    q_send(near[-1:])

    def z_peer(i):
        return (CORES * XH * ring(z, i, nz) + corner, col)

    @pl.loop(1, nz)
    def _(i):
        send(v_own.at[eight(ring(z, i, nz))], v_all.at[z, corner], V, z_peer(i)).start()

    pad = jnp.zeros((e_hi.shape[1], e_hi.shape[2] - width), bf16)
    for i in range(ny):
        e_hi[i, :, width:] = pad
        e_lo[i, :, width:] = pad
    q_cat[:, XL * block:] = jnp.zeros((r, q_cat.shape[1] - XL * block), f32)
    v_cat[:, block * nrow:] = jnp.zeros((GROUP, v_cat.shape[1] - block * nrow), f32)
    v_all[z, corner] = v_own[eight(z), :]
    for i in range(ny):
        convert(i)

    def rotate(i, first, last):
        at = pl.ds(first * pair, (last - first) * pair)
        share = folded(
            jnp.dot(x_cat[i], e_hi[i, :, at], preferred_element_type=f32)
            + jnp.dot(x_cat[i], e_lo[i, :, at], preferred_element_type=f32)
        )
        for j in range(first, last):
            for side in range(2):
                k = 2 * (j - first) + side
                part = share[:, k * LANES:(k + 1) * LANES]
                to = pl.ds(j * LANES, LANES)
                if i == 0:
                    rot[side, :, to] = part
                else:
                    rot[side, :, to] += part

    cuts = (0, chunks // 2 + 1, chunks)
    c_copies = []
    own_half = pl.ds(pl.multiple_of(core * (r // CORES), r // CORES), r // CORES)
    for i in range(ny):
        if i == ny - 1:
            all_in(v_all.at[pl.ds(0, nz - 1), corner], V)
            part = v_all.at[:, corner]
            for other in (partner, across, (across[0] + 1 - 2 * core, col)):
                send(part, part, V2, other).start()

            all_in(g_all.at[pl.ds(0, GROUP * (nt - 1))], G1)
            g_own[...] = g_all[...].T
            g_t[z, xh, own_half] = g_own[own_half, :]

            @pl.loop(1, nz)
            def _(k):
                part = g_t.at[z, xh, own_half]
                send(part, part, G2, z_peer(k)).start()

        place = ring(y, near[i], ny)
        if i == 0:
            there = q_all.at[pl.ds(XL * place + 1 - xl, 1)]
        else:
            there = q_all.at[pl.ds(XL * place, XL)]
        send(there, there, Q, partner, q_sem.at[i]).wait_recv()
        for side in range(XL):
            q_cat[:, side * block:(side + 1) * block] = q_all[XL * place + side]
        x_cat[i] = stacked(q_cat[...])
        for k in range(2):
            rotate(i, cuts[k], cuts[k + 1])
            if i == ny - 1:
                at = pl.ds(cuts[k] * LANES, (cuts[k + 1] - cuts[k]) * LANES)
                c_copies.append(
                    pltpu.make_async_remote_copy(
                        src_ref=rot.at[1 - core, :, at], dst_ref=rot_in.at[:, at], send_sem=c_sem.at[0, k],
                        recv_sem=c_sem.at[1, k], device_id=partner, device_id_type=MESH,
                    )
                )
                c_copies[k].start()

    lanes, halves = [], []
    for a, b in zip(cuts, cuts[1:]):
        middle = (a + b + 1) // 2
        lanes.append(pl.ds(a * LANES, (b - a) * LANES))
        halves.append((pl.ds(a * LANES, (middle - a) * LANES), pl.ds(middle * LANES, (b - middle) * LANES)))
    ways = ((1, 0), (nz - 1, 1))
    FIRST, MIDDLE, LAST, THROUGH = range(4)

    def z_send(src, dst, sent, landed, k, i):
        return pltpu.make_async_remote_copy(
            src_ref=src, dst_ref=dst, send_sem=z_sem.at[sent, k], recv_sem=z_sem.at[landed, k], device_id=z_peer(i),
            device_id_type=MESH,
        )

    for k, at in enumerate(lanes):
        c_copies[k].wait_recv()

        @pl.loop(0, nz)
        def _(i):
            mine[eight(i), at] = rot[core, eight(i), at] + rot_in[eight(i), at]

        for step, way in ways:
            part = halves[k][way]
            z_send(mine.at[eight(ring(z, nz // 2, nz)), part], z_far.at[way, :, part], FIRST, MIDDLE, k, 2 * step % nz).start()
        for step, way in ways:
            z_send(mine.at[eight(ring(z, 3 * step % nz, nz)), at], z_mid.at[way, :, at], FIRST, MIDDLE, k, step).start()

    for k, at in enumerate(lanes):
        for step, way in ways:
            z_send(mine.at[eight(ring(z, step, nz)), at], z_in.at[way, :, at], FIRST, LAST, k, step).start()

    def through(k):
        at = lanes[k]
        there = z_in.at[pl.ds(0, 3), :, at]
        z_send(there, there, FIRST, MIDDLE, k, 1).wait_recv()
        for step, way in ways:
            z_out[way, :, at] = mine[eight(ring(z, 2 * step % nz, nz)), at] + z_mid[way, :, at]
            z_out[way, :, halves[k][way]] += z_far[way, :, halves[k][way]]
        for step, way in ways:
            z_send(z_out.at[way, :, at], z_in.at[2 + way, :, at], THROUGH, LAST, k, 2 * step % nz).start()

    def transpose(first, last):
        @pl.loop(first, last)
        def _(j):
            at = pl.ds(pl.multiple_of(j * pair, pair), pair)
            to = pl.ds(pl.multiple_of(j * LANES, LANES), LANES)
            for i in range(ny):
                hi, lo = e_hi[i, :, at].T, e_lo[i, :, at].T
                for side in range(2):
                    t_hi[side, i, to, :] = hi[side * LANES:(side + 1) * LANES]
                    t_lo[side, i, to, :] = lo[side * LANES:(side + 1) * LANES]

    transpose(0, chunks * 3 // 4)
    for k in range(2):
        through(k)
    all_in(g_t.at[pl.ds(0, nz - 1), xh, own_half], G2)
    part = g_t.at[:, xh, own_half]
    send(part, part, G3, across).start()
    transpose(chunks * 3 // 4, chunks)

    def x_copy(k):
        at = lanes[k]
        return pltpu.make_async_remote_copy(
            src_ref=x_out.at[:, at], dst_ref=x_in.at[:, at], send_sem=x_sem.at[0, k], recv_sem=x_sem.at[1, k],
            device_id=across, device_id_type=MESH,
        )

    def ag_send(i, owner, at, k, kind):
        part = s_all.at[core, eight(owner), at]
        return send(part, part, AG, z_peer(i), ag_sem.at[k, kind])

    def fw_send(owner, at):
        part = s_all.at[core, eight(owner), at]
        return send(part, part, FW, partner)

    for k, at in enumerate(lanes):
        there = z_in.at[:, :, at]
        z_send(there, there, FIRST, LAST, k, 1).wait_recv()
        x_out[:, at] = mine[eight(z), at] + (z_in[0, :, at] + z_in[1, :, at]) + (z_in[2, :, at] + z_in[3, :, at])
        x_copy(k).start()

    all_in(v_all.at[:, pl.ds(0, CORES * XH - 1)], V2)
    for b in range(nrow):
        v_cat[:, b * block:(b + 1) * block] = v_all[b // (CORES * XH), b % (CORES * XH)]
    for j in range(2 * chunks):
        v_use[j % 2, :, (j // 2) * LANES:(j // 2 + 1) * LANES] = v_cat[:, j * LANES:(j + 1) * LANES]

    all_out(q_all.at[pl.ds(0, ncol - 1)], Q)
    all_out(g_all.at[pl.ds(0, GROUP * (nt - 1))], G1)
    all_out(v_all.at[pl.ds(0, nz - 1), corner], V)
    all_out(v_all.at[:, pl.ds(0, CORES * XH - 1)], V2)
    for copy in c_copies:
        copy.wait_send()
    for k, at in enumerate(lanes):
        there = mine.at[pl.ds(0, 5 * GROUP), at]
        z_send(there, there, FIRST, LAST, k, 1).wait_send()
        there = z_out.at[:, :, at]
        z_send(there, there, THROUGH, LAST, k, 1).wait_send()
    a_copy.wait()
    hi, lo = split(a_own[...])
    a_hi[...] = hi
    a_lo[...] = lo

    for k, at in enumerate(lanes):
        x_copy(k).wait()
        s_all[core, eight(z), at] = (x_out[:, at] + x_in[:, at]) / (v_use[core, :, at] + damping)
        for step, way in ways:
            ag_send(2 * step % nz, z, at, k, 2 + way).start()
        fw_send(z, at).start()

    for k, at in enumerate(lanes):
        for step, way in ways:
            ag_send(step, z, at, k, way).start()

    for k, at in enumerate(lanes):
        for step, way in ways:
            owner = ring(z, nz - 2 * step % nz, nz)
            ag_send(1, owner, at, k, 2 + way).wait_recv()
            ag_send(2 * step % nz, owner, halves[k][way], k, 6 + way).start()
            ag_send(step, owner, at, k, 4 + way).start()
            fw_send(owner, at).start()
        if k == 0:
            all_in(g_t.at[:, 1 - xh, own_half], G3)
            part = g_t.at[:, :, own_half]
            send(part, part, G4, partner).start()

    for k, at in enumerate(lanes):
        for away, kind in ((1, 0), (3, 4)):
            for step, way in ways:
                owner = ring(z, nz - away * step % nz, nz)
                ag_send(1, owner, at, k, kind + way).wait_recv()
                fw_send(owner, at).start()
        for step, way in ways:
            owner = ring(z, nz // 2, nz)
            ag_send(1, owner, halves[k][way], k, 6 + way).wait_recv()
            fw_send(owner, halves[k][way]).start()

    def back(side, i):
        return folded(
            jnp.dot(s_cat[side], t_hi[side, i], preferred_element_type=f32)
            + jnp.dot(s_cat[side], t_lo[side, i], preferred_element_type=f32)
        )

    s_cat[core] = stacked(s_all[core])
    for i in range(ny):
        p_own[i] = back(core, i)
    all_in(s_all.at[1 - core], FW)
    s_cat[1 - core] = stacked(s_all[1 - core])
    for group in ((3, 2), (1, 0)):
        for i in group:
            part = p_own[i] + back(1 - core, i)
            for side in range(XL):
                p_out[i, side] = part[:, side * block:(side + 1) * block]
        for i in group:
            if i == 0:
                send(p_out.at[0, 1 - xl], p_in.at[col], P_, (row, col + 1 - 2 * xl)).start()
            else:
                place = ring(y, near[i], ny)
                for side in range(XL):
                    send(p_out.at[i, side], p_in.at[col], P_, (row, XL * place + side)).start()

    all_in(g_t.at[:, :, pl.ds(pl.multiple_of((1 - core) * (r // CORES), r // CORES), r // CORES)], G4)
    all_out(g_t.at[pl.ds(0, nz - 1), xh, own_half], G2)
    all_out(s_all.at[core, pl.ds(0, GROUP * (nz - 1))], AG)
    all_out(s_all.at[core], FW)
    all_out(g_t.at[:, xh, own_half], G3)
    all_out(g_t.at[:, :, own_half], G4)

    all_in(p_in.at[pl.ds(0, ncol - 1)], P_)
    whole = lax.fori_loop(1, ncol, lambda i, total: total + p_in[ring(col, i, ncol)], p_out[0, xl])
    p_ref[...] = whole

    x = stacked(whole)
    for k in range(nchip // 2):
        at = slice(k * pair, (k + 1) * pair)
        projected = folded(
            jnp.dot(x, a_hi[:, at], preferred_element_type=f32) + jnp.dot(x, a_lo[:, at], preferred_element_type=f32)
        )
        for side in range(2):
            there = 2 * k + side
            part = projected[:, side * LANES:(side + 1) * LANES] * g_t[there // XH, there % XH]
            f_out[there // XH, there % XH] = jnp.sum(part, axis=0, keepdims=True)

    place, nplace = CORES * z + core, CORES * nz

    @pl.loop(1, nplace)
    def _(i):
        to = ring(place, i, nplace)
        there = lax.div(to, CORES)
        send(f_out.at[there], f_in.at[place], F1, (CORES * (XH * there + xh) + lax.rem(to, CORES), col)).start()

    all_out(p_in.at[pl.ds(0, ncol - 1)], P_)
    all_in(f_in.at[pl.ds(0, nplace - 1)], F1)
    f_sum[...] = lax.fori_loop(1, nplace, lambda i, total: total + f_in[ring(place, i, nplace)], f_out[z])

    spot, nspot = ncol * xh + col, XH * ncol

    @pl.loop(1, nspot)
    def _(i):
        to = ring(spot, i, nspot)
        there = lax.div(to, ncol)
        send(f_sum.at[there], f_all.at[spot], F2, (CORES * (XH * z + there) + core, lax.rem(to, ncol))).start()

    all_out(f_in.at[pl.ds(0, nplace - 1)], F1)
    all_in(f_all.at[pl.ds(0, nspot - 1)], F2)
    total = lax.fori_loop(1, nspot, lambda i, total: total + f_all[ring(spot, i, nspot)], f_sum[xh])
    total = jnp.broadcast_to(total, (GROUP, LANES))
    s_ref[...] = pltpu.roll(total, lax.rem(LANES - GROUP * t, LANES), axis=1)
    all_out(f_all.at[pl.ds(0, nspot - 1)], F2)


def shards(nrow, ncol, query_slab, eigenbasis, eigenvalues, activations, out_grads):
    depth, width = eigenbasis.shape
    block, r = query_slab.shape
    ntrain = activations.shape[0]
    nchip, nz, ny, nt = nrow // CORES, nrow // (CORES * XH), ncol // XL, CORES * ncol
    wide = pl.cdiv(width, 2 * LANES) * 2 * LANES
    half = wide // 2
    rows = depth // ny
    deep = pl.cdiv(rows, 16) * 16
    v, dma = pltpu.VMEM, pltpu.SemaphoreType.DMA
    anywhere, vmem = pl.BlockSpec(memory_space=pl.ANY), pl.BlockSpec(memory_space=pltpu.VMEM)
    scratch = [
        v((ny, rows, width), f32), v((ny, deep, wide), bf16), v((ny, deep, wide), bf16),
        v((2, ny, half, deep), bf16), v((2, ny, half, deep), bf16),
        v((ncol, r, block), f32), v((r, deep), f32), v((ny, 2 * r, deep), bf16),
        v((2, r, half), f32), v((r, half), f32), v((r, half), f32),
        v((2, GROUP, half), f32), v((2, GROUP, half), f32), v((2, GROUP, half), f32), v((4, GROUP, half), f32),
        v((GROUP, half), f32), v((GROUP, half), f32),
        v((r, block), f32), v((nz, CORES * XH, GROUP, block), f32), v((GROUP, wide), f32), v((2, GROUP, half), f32),
        v((2, r, half), f32), v((2, 2 * r, half), bf16), v((ny, r, deep), f32),
        v((ny, XL, r, block), f32), v((ncol, r, block), f32),
        v((block, ntrain), f32), v((block, ntrain), bf16), v((block, ntrain), bf16),
        v((GROUP * nt, r), f32), v((r, LANES), f32), v((nz, XH, r, LANES), f32),
        v((nz, XH, 1, LANES), f32), v((CORES * nz, XH, 1, LANES), f32), v((XH, 1, LANES), f32), v((nt, 1, LANES), f32),
        dma((ny,)), dma((4,)), dma((2, 12)), dma((ny,)), dma((2, 2)), dma((4, 2)), dma((2, 2)), dma((2, 8)),
    ]
    preconditioned, scores = pl.pallas_call(
        functools.partial(kernel, nrow, ncol),
        out_shape=(pltpu.VMEM((r, block), f32), pltpu.VMEM((GROUP, LANES), f32)),
        in_specs=[anywhere] * 5,
        out_specs=(vmem, vmem),
        scratch_shapes=scratch,
        compiler_params=pltpu.CompilerParams(collective_id=0, has_side_effects=True, vmem_limit_bytes=60 * 2**20),
    )(query_slab.T, eigenbasis, eigenvalues.T, activations.T, out_grads)
    return preconditioned.T, scores[0, :GROUP]


def solution(mesh):
    return jax.shard_map(
        functools.partial(shards, mesh.shape["row"], mesh.shape["col"]),
        mesh=mesh,
        in_specs=(
            P(("row", "col"), None),
            P("row", "col"),
            P(("col", "row"), None),
            P(None, ("row", "col")),
            P(("row", "col"), None),
        ),
        out_specs=(P(("row", "col"), None), P(("row", "col"))),
        check_vma=False,
    )
```

```python
import functools

import jax
import jax.numpy as jnp
from jax import lax
from jax.experimental import pallas as pl
from jax.experimental.pallas import tpu as pltpu
from jax.sharding import PartitionSpec as P

damping = 0.1
MESH = pl.DeviceIdType.MESH
f32, bf16 = jnp.float32, jnp.bfloat16
LANES, GROUP = 128, 8
CORES = XH = 2
XL = 2


def split(x):
    hi = x.astype(bf16)
    return hi, (x - hi.astype(f32)).astype(bf16)


def stacked(x):
    return jnp.concatenate(split(x), axis=0)


def folded(x):
    half = x.shape[0] // 2
    return x[:half] + x[half:]


def kernel(
    nrow, ncol,
    q_ref, e_ref, v_ref, a_ref, g_ref,
    p_ref, s_ref,
    stage, e_hi, e_lo, t_hi, t_lo, q_all, q_cat, x_cat, rot, rot_in, mine, z_far, z_mid, z_out, z_in, x_out, x_in,
    v_own, v_all, v_cat, v_use, s_all, s_cat, p_own, p_out, p_in,
    a_own, a_hi, a_lo, g_all, g_own, g_t, f_out, f_in, f_sum, f_all,
    e_sem, local, one_sem, v_sem, q_sem, c_sem, z_sem, x_sem, ag_sem,
):
    row, col = lax.axis_index("row"), lax.axis_index("col")
    core, chip = lax.rem(row, CORES), lax.div(row, CORES)
    xh, z = lax.rem(chip, XH), lax.div(chip, XH)
    xl, y = lax.rem(col, XL), lax.div(col, XL)
    nchip, nz, ny, nt = nrow // CORES, nrow // (CORES * XH), ncol // XL, CORES * ncol
    t = core * ncol + col
    depth, width = e_ref.shape
    r, block = q_ref.shape
    half = rot.shape[2]
    chunks = half // LANES
    pair = 2 * LANES
    rows = depth // ny
    partner = (row + 1 - 2 * core, col)
    across = (row + 2 - 4 * xh, col)
    near = sorted(range(ny), key=lambda d: min(d, ny - d))
    Q, G1, V, V2, AG, FW, G2, G3, G4, P_, F1, F2 = range(12)
    corner = XH * xh + core

    def send(src, dst, kind, device, recv=None):
        return pltpu.make_async_remote_copy(
            src_ref=src, dst_ref=dst, send_sem=one_sem.at[0, kind], recv_sem=one_sem.at[1, kind] if recv is None else recv,
            device_id=device, device_id_type=MESH,
        )

    def all_in(ref, kind):
        send(ref, ref, kind, partner).wait_recv()

    def all_out(ref, kind):
        send(ref, ref, kind, partner).wait_send()

    def ring(place, i, n):
        return lax.rem(place + i, n)

    def eight(k):
        return pl.ds(pl.multiple_of(GROUP * k, GROUP), GROUP)

    def e_copy(i):
        at = pl.ds(pl.multiple_of(rows * ring(y, near[i], ny), GROUP), rows)
        return pltpu.make_async_copy(e_ref.at[at], stage.at[i], e_sem.at[i])

    q_copy = pltpu.make_async_copy(q_ref, q_all.at[col], local.at[0])
    g_copy = pltpu.make_async_copy(g_ref, g_all.at[eight(t)], local.at[1])
    v_copy = pltpu.make_async_copy(v_ref, v_own, local.at[2])
    a_copy = pltpu.make_async_copy(a_ref, a_own, local.at[3])
    q_copy.start()
    g_copy.start()
    v_copy.start()
    for i in range(ny):
        e_copy(i).start()
    a_copy.start()

    barrier = pltpu.get_barrier_semaphore()
    diagonal = (across[0] + 1 - 2 * core, col)

    def z_peer(i):
        return (CORES * XH * ring(z, i, nz) + corner, col)

    close = (1, nz - 1, 2, nz - 2)

    @pl.loop(1, ncol)
    def _(i):
        other = ring(col, i, ncol)
        pl.semaphore_signal(barrier, inc=1, device_id=(row, other), device_id_type=MESH)
        pl.semaphore_signal(barrier, inc=1, device_id=(partner[0], other), device_id_type=MESH)

    for device in (*(z_peer(i) for i in close), across, diagonal, partner):
        pl.semaphore_signal(barrier, inc=1, device_id=device, device_id_type=MESH)

    def convert(i):
        e_copy(i).wait()

        def put(at, x):
            hi, lo = split(x)
            e_hi[i, at, :width] = hi
            e_lo[i, at, :width] = lo

        @pl.loop(0, rows // 16)
        def _(k):
            at = pl.ds(pl.multiple_of(k * 16, 16), 16)
            put(at, stage[i, at, :])

        done = rows // 16 * 16
        left = jnp.concatenate([stage[i, done:, :], jnp.zeros((e_hi.shape[1] - rows, width), f32)], axis=0)
        put(slice(done, None), left)

    q_copy.wait()
    g_copy.wait()
    v_copy.wait()
    pl.semaphore_wait(barrier, 2 * (ncol - 1) + len(close) + 3)

    own_q = q_all.at[col]
    send(own_q, own_q, Q, (row, col + 1 - 2 * xl), q_sem.at[0]).start()

    def q_send(places):
        for d in places:
            slot = near.index(ny - d)
            for side in range(XL):
                send(own_q, own_q, Q, (row, XL * ring(y, d, ny) + side), q_sem.at[slot]).start()

    q_send(near[1:-1])

    @pl.loop(1, nt)
    def _(i):
        to = ring(t, i, nt)
        part = g_all.at[eight(t)]
        send(part, part, G1, (CORES * chip + lax.div(to, ncol), lax.rem(to, ncol))).start()

    q_send(near[-1:])

    def v_send(i, owner):
        return send(v_own.at[eight(ring(z, i, nz))], v_all.at[owner, corner], V, z_peer(i))

    def near_v(i, owner):
        return send(v_own.at[eight(ring(z, i, nz))], v_all.at[owner, corner], V, z_peer(i), v_sem.at[close.index(i)])

    for i in close:
        near_v(i, z).start()

    pad = jnp.zeros((e_hi.shape[1], e_hi.shape[2] - width), bf16)
    for i in range(ny):
        e_hi[i, :, width:] = pad
        e_lo[i, :, width:] = pad
    q_cat[:, XL * block:] = jnp.zeros((r, q_cat.shape[1] - XL * block), f32)
    v_cat[:, block * nrow:] = jnp.zeros((GROUP, v_cat.shape[1] - block * nrow), f32)
    v_all[z, corner] = v_own[eight(z), :]
    for i in range(ny):
        convert(i)

    def rotate(i, first, last):
        at = pl.ds(first * pair, (last - first) * pair)
        share = folded(
            jnp.dot(x_cat[i], e_hi[i, :, at], preferred_element_type=f32)
            + jnp.dot(x_cat[i], e_lo[i, :, at], preferred_element_type=f32)
        )
        for j in range(first, last):
            for side in range(2):
                k = 2 * (j - first) + side
                part = share[:, k * LANES:(k + 1) * LANES]
                to = pl.ds(j * LANES, LANES)
                if i == 0:
                    rot[side, :, to] = part
                else:
                    rot[side, :, to] += part

    cuts = (0, chunks // 2 + 1, chunks)
    c_copies = []
    own_half = pl.ds(pl.multiple_of(core * (r // CORES), r // CORES), r // CORES)
    for i in range(ny):
        if i == ny - 1:
            all_in(g_all.at[pl.ds(0, GROUP * (nt - 1))], G1)
            g_own[...] = g_all[...].T
            g_t[z, xh, own_half] = g_own[own_half, :]

            @pl.loop(1, nz)
            def _(k):
                part = g_t.at[z, xh, own_half]
                send(part, part, G2, z_peer(k)).start()

        place = ring(y, near[i], ny)
        if i == 0:
            there = q_all.at[pl.ds(XL * place + 1 - xl, 1)]
        else:
            there = q_all.at[pl.ds(XL * place, XL)]
        send(there, there, Q, partner, q_sem.at[i]).wait_recv()
        for side in range(XL):
            q_cat[:, side * block:(side + 1) * block] = q_all[XL * place + side]
        x_cat[i] = stacked(q_cat[...])
        if i == 0:
            for k in close:
                near_v(k, ring(z, nz - k, nz)).wait_recv()
            for k in range(3, nz - 2):
                v_send(k, z).start()

        for k in range(2):
            rotate(i, cuts[k], cuts[k + 1])
            if i == ny - 1:
                at = pl.ds(cuts[k] * LANES, (cuts[k + 1] - cuts[k]) * LANES)
                c_copies.append(
                    pltpu.make_async_remote_copy(
                        src_ref=rot.at[1 - core, :, at], dst_ref=rot_in.at[:, at], send_sem=c_sem.at[0, k],
                        recv_sem=c_sem.at[1, k], device_id=partner, device_id_type=MESH,
                    )
                )
                c_copies[k].start()

    lanes, halves = [], []
    for a, b in zip(cuts, cuts[1:]):
        middle = (a + b + 1) // 2
        lanes.append(pl.ds(a * LANES, (b - a) * LANES))
        halves.append((pl.ds(a * LANES, (middle - a) * LANES), pl.ds(middle * LANES, (b - middle) * LANES)))
    ways = ((1, 0), (nz - 1, 1))
    FIRST, MIDDLE, LAST, THROUGH = range(4)

    def z_send(src, dst, sent, landed, k, i):
        return pltpu.make_async_remote_copy(
            src_ref=src, dst_ref=dst, send_sem=z_sem.at[sent, k], recv_sem=z_sem.at[landed, k], device_id=z_peer(i),
            device_id_type=MESH,
        )

    for k, at in enumerate(lanes):
        c_copies[k].wait_recv()

        @pl.loop(0, nz)
        def _(i):
            mine[eight(i), at] = rot[core, eight(i), at] + rot_in[eight(i), at]

        for step, way in ways:
            part = halves[k][way]
            z_send(mine.at[eight(ring(z, nz // 2, nz)), part], z_far.at[way, :, part], FIRST, MIDDLE, k, 2 * step % nz).start()
        for step, way in ways:
            z_send(mine.at[eight(ring(z, 3 * step % nz, nz)), at], z_mid.at[way, :, at], FIRST, MIDDLE, k, step).start()

    for k, at in enumerate(lanes):
        for step, way in ways:
            z_send(mine.at[eight(ring(z, step, nz)), at], z_in.at[way, :, at], FIRST, LAST, k, step).start()

    def through(k):
        at = lanes[k]
        there = z_in.at[pl.ds(0, 3), :, at]
        z_send(there, there, FIRST, MIDDLE, k, 1).wait_recv()
        for step, way in ways:
            z_out[way, :, at] = mine[eight(ring(z, 2 * step % nz, nz)), at] + z_mid[way, :, at]
            z_out[way, :, halves[k][way]] += z_far[way, :, halves[k][way]]
        for step, way in ways:
            z_send(z_out.at[way, :, at], z_in.at[2 + way, :, at], THROUGH, LAST, k, 2 * step % nz).start()

    def transpose(first, last):
        @pl.loop(first, last)
        def _(j):
            at = pl.ds(pl.multiple_of(j * pair, pair), pair)
            to = pl.ds(pl.multiple_of(j * LANES, LANES), LANES)
            for i in range(ny):
                hi, lo = e_hi[i, :, at].T, e_lo[i, :, at].T
                for side in range(2):
                    t_hi[side, i, to, :] = hi[side * LANES:(side + 1) * LANES]
                    t_lo[side, i, to, :] = lo[side * LANES:(side + 1) * LANES]

    all_in(v_all.at[pl.ds(0, nz - 1 - len(close)), corner], V)
    part = v_all.at[:, corner]
    for other in (partner, across, diagonal):
        send(part, part, V2, other).start()

    transpose(0, chunks * 3 // 4)
    for k in range(2):
        through(k)
    all_in(g_t.at[pl.ds(0, nz - 1), xh, own_half], G2)
    part = g_t.at[:, xh, own_half]
    send(part, part, G3, across).start()
    transpose(chunks * 3 // 4, chunks)

    def x_copy(k):
        at = lanes[k]
        return pltpu.make_async_remote_copy(
            src_ref=x_out.at[:, at], dst_ref=x_in.at[:, at], send_sem=x_sem.at[0, k], recv_sem=x_sem.at[1, k],
            device_id=across, device_id_type=MESH,
        )

    def ag_send(i, owner, at, k, kind):
        part = s_all.at[core, eight(owner), at]
        return send(part, part, AG, z_peer(i), ag_sem.at[k, kind])

    def fw_send(owner, at):
        part = s_all.at[core, eight(owner), at]
        return send(part, part, FW, partner)

    for k, at in enumerate(lanes):
        there = z_in.at[:, :, at]
        z_send(there, there, FIRST, LAST, k, 1).wait_recv()
        x_out[:, at] = mine[eight(z), at] + (z_in[0, :, at] + z_in[1, :, at]) + (z_in[2, :, at] + z_in[3, :, at])
        x_copy(k).start()

    all_in(v_all.at[:, pl.ds(0, CORES * XH - 1)], V2)
    for b in range(nrow):
        v_cat[:, b * block:(b + 1) * block] = v_all[b // (CORES * XH), b % (CORES * XH)]
    for j in range(2 * chunks):
        v_use[j % 2, :, (j // 2) * LANES:(j // 2 + 1) * LANES] = v_cat[:, j * LANES:(j + 1) * LANES]

    all_out(q_all.at[pl.ds(0, ncol - 1)], Q)
    all_out(g_all.at[pl.ds(0, GROUP * (nt - 1))], G1)
    all_out(v_all.at[pl.ds(0, nz - 1), corner], V)
    all_out(v_all.at[:, pl.ds(0, CORES * XH - 1)], V2)
    for copy in c_copies:
        copy.wait_send()
    for k, at in enumerate(lanes):
        there = mine.at[pl.ds(0, 5 * GROUP), at]
        z_send(there, there, FIRST, LAST, k, 1).wait_send()
        there = z_out.at[:, :, at]
        z_send(there, there, THROUGH, LAST, k, 1).wait_send()
    a_copy.wait()
    hi, lo = split(a_own[...])
    a_hi[...] = hi
    a_lo[...] = lo

    for k, at in enumerate(lanes):
        x_copy(k).wait()
        s_all[core, eight(z), at] = (x_out[:, at] + x_in[:, at]) / (v_use[core, :, at] + damping)
        for step, way in ways:
            ag_send(2 * step % nz, z, at, k, 2 + way).start()
        fw_send(z, at).start()

    for k, at in enumerate(lanes):
        for step, way in ways:
            ag_send(step, z, at, k, way).start()

    for k, at in enumerate(lanes):
        for step, way in ways:
            owner = ring(z, nz - 2 * step % nz, nz)
            ag_send(1, owner, at, k, 2 + way).wait_recv()
            ag_send(2 * step % nz, owner, halves[k][way], k, 6 + way).start()
            ag_send(step, owner, at, k, 4 + way).start()
            fw_send(owner, at).start()
        if k == 0:
            all_in(g_t.at[:, 1 - xh, own_half], G3)
            part = g_t.at[:, :, own_half]
            send(part, part, G4, partner).start()

    for k, at in enumerate(lanes):
        for away, kind in ((1, 0), (3, 4)):
            for step, way in ways:
                owner = ring(z, nz - away * step % nz, nz)
                ag_send(1, owner, at, k, kind + way).wait_recv()
                fw_send(owner, at).start()
        for step, way in ways:
            owner = ring(z, nz // 2, nz)
            ag_send(1, owner, halves[k][way], k, 6 + way).wait_recv()
            fw_send(owner, halves[k][way]).start()

    def back(side, i):
        return folded(
            jnp.dot(s_cat[side], t_hi[side, i], preferred_element_type=f32)
            + jnp.dot(s_cat[side], t_lo[side, i], preferred_element_type=f32)
        )

    s_cat[core] = stacked(s_all[core])
    for i in range(ny):
        p_own[i] = back(core, i)
    all_in(s_all.at[1 - core], FW)
    s_cat[1 - core] = stacked(s_all[1 - core])
    for group in ((3, 2), (1, 0)):
        for i in group:
            part = p_own[i] + back(1 - core, i)
            for side in range(XL):
                p_out[i, side] = part[:, side * block:(side + 1) * block]
        for i in group:
            if i == 0:
                send(p_out.at[0, 1 - xl], p_in.at[col], P_, (row, col + 1 - 2 * xl)).start()
            else:
                place = ring(y, near[i], ny)
                for side in range(XL):
                    send(p_out.at[i, side], p_in.at[col], P_, (row, XL * place + side)).start()

    all_in(g_t.at[:, :, pl.ds(pl.multiple_of((1 - core) * (r // CORES), r // CORES), r // CORES)], G4)
    all_out(g_t.at[pl.ds(0, nz - 1), xh, own_half], G2)
    all_out(s_all.at[core, pl.ds(0, GROUP * (nz - 1))], AG)
    all_out(s_all.at[core], FW)
    all_out(g_t.at[:, xh, own_half], G3)
    all_out(g_t.at[:, :, own_half], G4)

    all_in(p_in.at[pl.ds(0, ncol - 1)], P_)
    whole = lax.fori_loop(1, ncol, lambda i, total: total + p_in[ring(col, i, ncol)], p_out[0, xl])
    p_ref[...] = whole

    x = stacked(whole)
    for k in range(nchip // 2):
        at = slice(k * pair, (k + 1) * pair)
        projected = folded(
            jnp.dot(x, a_hi[:, at], preferred_element_type=f32) + jnp.dot(x, a_lo[:, at], preferred_element_type=f32)
        )
        for side in range(2):
            there = 2 * k + side
            part = projected[:, side * LANES:(side + 1) * LANES] * g_t[there // XH, there % XH]
            f_out[there // XH, there % XH] = jnp.sum(part, axis=0, keepdims=True)

    place, nplace = CORES * z + core, CORES * nz

    @pl.loop(1, nplace)
    def _(i):
        to = ring(place, i, nplace)
        there = lax.div(to, CORES)
        send(f_out.at[there], f_in.at[place], F1, (CORES * (XH * there + xh) + lax.rem(to, CORES), col)).start()

    all_out(p_in.at[pl.ds(0, ncol - 1)], P_)
    all_in(f_in.at[pl.ds(0, nplace - 1)], F1)
    f_sum[...] = lax.fori_loop(1, nplace, lambda i, total: total + f_in[ring(place, i, nplace)], f_out[z])

    spot, nspot = ncol * xh + col, XH * ncol

    @pl.loop(1, nspot)
    def _(i):
        to = ring(spot, i, nspot)
        there = lax.div(to, ncol)
        send(f_sum.at[there], f_all.at[spot], F2, (CORES * (XH * z + there) + core, lax.rem(to, ncol))).start()

    all_out(f_in.at[pl.ds(0, nplace - 1)], F1)
    all_in(f_all.at[pl.ds(0, nspot - 1)], F2)
    total = lax.fori_loop(1, nspot, lambda i, total: total + f_all[ring(spot, i, nspot)], f_sum[xh])
    total = jnp.broadcast_to(total, (GROUP, LANES))
    s_ref[...] = pltpu.roll(total, lax.rem(LANES - GROUP * t, LANES), axis=1)
    all_out(f_all.at[pl.ds(0, nspot - 1)], F2)


def shards(nrow, ncol, query_slab, eigenbasis, eigenvalues, activations, out_grads):
    depth, width = eigenbasis.shape
    block, r = query_slab.shape
    ntrain = activations.shape[0]
    nchip, nz, ny, nt = nrow // CORES, nrow // (CORES * XH), ncol // XL, CORES * ncol
    wide = pl.cdiv(width, 2 * LANES) * 2 * LANES
    half = wide // 2
    rows = depth // ny
    deep = pl.cdiv(rows, 16) * 16
    v, dma = pltpu.VMEM, pltpu.SemaphoreType.DMA
    anywhere, vmem = pl.BlockSpec(memory_space=pl.ANY), pl.BlockSpec(memory_space=pltpu.VMEM)
    scratch = [
        v((ny, rows, width), f32), v((ny, deep, wide), bf16), v((ny, deep, wide), bf16),
        v((2, ny, half, deep), bf16), v((2, ny, half, deep), bf16),
        v((ncol, r, block), f32), v((r, deep), f32), v((ny, 2 * r, deep), bf16),
        v((2, r, half), f32), v((r, half), f32), v((r, half), f32),
        v((2, GROUP, half), f32), v((2, GROUP, half), f32), v((2, GROUP, half), f32), v((4, GROUP, half), f32),
        v((GROUP, half), f32), v((GROUP, half), f32),
        v((r, block), f32), v((nz, CORES * XH, GROUP, block), f32), v((GROUP, wide), f32), v((2, GROUP, half), f32),
        v((2, r, half), f32), v((2, 2 * r, half), bf16), v((ny, r, deep), f32),
        v((ny, XL, r, block), f32), v((ncol, r, block), f32),
        v((block, ntrain), f32), v((block, ntrain), bf16), v((block, ntrain), bf16),
        v((GROUP * nt, r), f32), v((r, LANES), f32), v((nz, XH, r, LANES), f32),
        v((nz, XH, 1, LANES), f32), v((CORES * nz, XH, 1, LANES), f32), v((XH, 1, LANES), f32), v((nt, 1, LANES), f32),
        dma((ny,)), dma((4,)), dma((2, 12)), dma((4,)), dma((ny,)), dma((2, 2)), dma((4, 2)), dma((2, 2)), dma((2, 8)),
    ]
    preconditioned, scores = pl.pallas_call(
        functools.partial(kernel, nrow, ncol),
        out_shape=(pltpu.VMEM((r, block), f32), pltpu.VMEM((GROUP, LANES), f32)),
        in_specs=[anywhere] * 5,
        out_specs=(vmem, vmem),
        scratch_shapes=scratch,
        compiler_params=pltpu.CompilerParams(collective_id=0, has_side_effects=True, vmem_limit_bytes=60 * 2**20),
    )(query_slab.T, eigenbasis, eigenvalues.T, activations.T, out_grads)
    return preconditioned.T, scores[0, :GROUP]


def solution(mesh):
    return jax.shard_map(
        functools.partial(shards, mesh.shape["row"], mesh.shape["col"]),
        mesh=mesh,
        in_specs=(
            P(("row", "col"), None),
            P("row", "col"),
            P(("col", "row"), None),
            P(None, ("row", "col")),
            P(("row", "col"), None),
        ),
        out_specs=(P(("row", "col"), None), P(("row", "col"))),
        check_vma=False,
    )
```

```python
import functools

import jax
import jax.numpy as jnp
from jax import lax
from jax.experimental import pallas as pl
from jax.experimental.pallas import tpu as pltpu
from jax.sharding import PartitionSpec as P

damping = 0.1
MESH = pl.DeviceIdType.MESH
f32, bf16 = jnp.float32, jnp.bfloat16
LANES, GROUP = 128, 8
CHUNKS = 3
CORES = XH = 2
XL = 2


def split(x):
    hi = x.astype(bf16)
    return hi, (x - hi.astype(f32)).astype(bf16)


def stacked(x):
    return jnp.concatenate(split(x), axis=0)


def folded(x):
    half = x.shape[0] // 2
    return x[:half] + x[half:]


def kernel(
    nrow, ncol,
    q_ref, e_ref, v_ref, a_ref, g_ref,
    p_ref, s_ref,
    stage, e_hi, e_lo, t_hi, t_lo, q_all, q_cat, x_cat, rot, rot_in, mine, z_far, z_mid, z_out, z_in, x_out, x_in,
    v_own, v_all, v_cat, v_use, s_all, s_cat, p_own, p_out, p_in,
    a_own, a_hi, a_lo, g_all, g_own, g_t, f_out, f_in, f_sum, f_all,
    e_sem, local, one_sem, v_sem, q_sem, c_sem, z_sem, x_sem, ag_sem,
):
    row, col = lax.axis_index("row"), lax.axis_index("col")
    core, chip = lax.rem(row, CORES), lax.div(row, CORES)
    xh, z = lax.rem(chip, XH), lax.div(chip, XH)
    xl, y = lax.rem(col, XL), lax.div(col, XL)
    nchip, nz, ny, nt = nrow // CORES, nrow // (CORES * XH), ncol // XL, CORES * ncol
    t = core * ncol + col
    depth, width = e_ref.shape
    r, block = q_ref.shape
    half = rot.shape[2]
    chunks = half // LANES
    pair = 2 * LANES
    rows = depth // ny
    partner = (row + 1 - 2 * core, col)
    across = (row + 2 - 4 * xh, col)
    near = sorted(range(ny), key=lambda d: min(d, ny - d))
    Q, G1, V, V2, AG, FW, FW_LAST, G2, G3, G4, P_, F1, F2 = range(13)
    corner = XH * xh + core

    def send(src, dst, kind, device, recv=None):
        return pltpu.make_async_remote_copy(
            src_ref=src, dst_ref=dst, send_sem=one_sem.at[0, kind], recv_sem=one_sem.at[1, kind] if recv is None else recv,
            device_id=device, device_id_type=MESH,
        )

    def all_in(ref, kind):
        send(ref, ref, kind, partner).wait_recv()

    def all_out(ref, kind):
        send(ref, ref, kind, partner).wait_send()

    def ring(place, i, n):
        return lax.rem(place + i, n)

    def eight(k):
        return pl.ds(pl.multiple_of(GROUP * k, GROUP), GROUP)

    def e_copy(i):
        at = pl.ds(pl.multiple_of(rows * ring(y, near[i], ny), GROUP), rows)
        return pltpu.make_async_copy(e_ref.at[at], stage.at[i], e_sem.at[i])

    q_copy = pltpu.make_async_copy(q_ref, q_all.at[col], local.at[0])
    g_copy = pltpu.make_async_copy(g_ref, g_all.at[eight(t)], local.at[1])
    v_copy = pltpu.make_async_copy(v_ref, v_own, local.at[2])
    a_copy = pltpu.make_async_copy(a_ref, a_own, local.at[3])
    q_copy.start()
    g_copy.start()
    v_copy.start()
    for i in range(ny):
        e_copy(i).start()
    a_copy.start()

    barrier = pltpu.get_barrier_semaphore()
    diagonal = (across[0] + 1 - 2 * core, col)

    def z_peer(i):
        return (CORES * XH * ring(z, i, nz) + corner, col)

    close = (1, nz - 1, 2, nz - 2)

    @pl.loop(1, ncol)
    def _(i):
        other = ring(col, i, ncol)
        pl.semaphore_signal(barrier, inc=1, device_id=(row, other), device_id_type=MESH)
        pl.semaphore_signal(barrier, inc=1, device_id=(partner[0], other), device_id_type=MESH)

    for device in (*(z_peer(i) for i in close), across, diagonal, partner):
        pl.semaphore_signal(barrier, inc=1, device_id=device, device_id_type=MESH)

    def convert(i):
        e_copy(i).wait()

        def put(at, x):
            hi, lo = split(x)
            e_hi[i, at, :width] = hi
            e_lo[i, at, :width] = lo

        @pl.loop(0, rows // 16)
        def _(k):
            at = pl.ds(pl.multiple_of(k * 16, 16), 16)
            put(at, stage[i, at, :])

        done = rows // 16 * 16
        left = jnp.concatenate([stage[i, done:, :], jnp.zeros((e_hi.shape[1] - rows, width), f32)], axis=0)
        put(slice(done, None), left)

    q_copy.wait()
    g_copy.wait()
    v_copy.wait()
    pl.semaphore_wait(barrier, 2 * (ncol - 1) + len(close) + 3)

    own_q = q_all.at[col]
    send(own_q, own_q, Q, (row, col + 1 - 2 * xl), q_sem.at[0]).start()

    def q_send(places):
        for d in places:
            slot = near.index(ny - d)
            for side in range(XL):
                send(own_q, own_q, Q, (row, XL * ring(y, d, ny) + side), q_sem.at[slot]).start()

    q_send(near[1:-1])

    @pl.loop(1, nt)
    def _(i):
        to = ring(t, i, nt)
        part = g_all.at[eight(t)]
        send(part, part, G1, (CORES * chip + lax.div(to, ncol), lax.rem(to, ncol))).start()

    q_send(near[-1:])

    def v_send(i, owner):
        return send(v_own.at[eight(ring(z, i, nz))], v_all.at[owner, corner], V, z_peer(i))

    def near_v(i, owner):
        return send(v_own.at[eight(ring(z, i, nz))], v_all.at[owner, corner], V, z_peer(i), v_sem.at[close.index(i)])

    for i in close:
        near_v(i, z).start()

    pad = jnp.zeros((e_hi.shape[1], e_hi.shape[2] - width), bf16)
    for i in range(ny):
        e_hi[i, :, width:] = pad
        e_lo[i, :, width:] = pad
    q_cat[:, XL * block:] = jnp.zeros((r, q_cat.shape[1] - XL * block), f32)
    v_cat[:, block * nrow:] = jnp.zeros((GROUP, v_cat.shape[1] - block * nrow), f32)
    v_all[z, corner] = v_own[eight(z), :]
    for i in range(ny):
        convert(i)

    def rotate(i, first, last):
        at = pl.ds(first * pair, (last - first) * pair)
        share = folded(
            jnp.dot(x_cat[i], e_hi[i, :, at], preferred_element_type=f32)
            + jnp.dot(x_cat[i], e_lo[i, :, at], preferred_element_type=f32)
        )
        for j in range(first, last):
            for side in range(2):
                k = 2 * (j - first) + side
                part = share[:, k * LANES:(k + 1) * LANES]
                to = pl.ds(j * LANES, LANES)
                if i == 0:
                    rot[side, :, to] = part
                else:
                    rot[side, :, to] += part

    cuts = [-(-chunks * k // CHUNKS) for k in range(CHUNKS + 1)]
    c_copies = []
    own_half = pl.ds(pl.multiple_of(core * (r // CORES), r // CORES), r // CORES)
    for i in range(ny):
        place = ring(y, near[i], ny)
        if i == 0:
            there = q_all.at[pl.ds(XL * place + 1 - xl, 1)]
        else:
            there = q_all.at[pl.ds(XL * place, XL)]
        send(there, there, Q, partner, q_sem.at[i]).wait_recv()
        for side in range(XL):
            q_cat[:, side * block:(side + 1) * block] = q_all[XL * place + side]
        x_cat[i] = stacked(q_cat[...])
        if i == 0:
            for k in close:
                near_v(k, ring(z, nz - k, nz)).wait_recv()
            for k in range(3, nz - 2):
                v_send(k, z).start()

        for k in range(len(cuts) - 1):
            rotate(i, cuts[k], cuts[k + 1])
            if i == ny - 1:
                at = pl.ds(cuts[k] * LANES, (cuts[k + 1] - cuts[k]) * LANES)
                c_copies.append(
                    pltpu.make_async_remote_copy(
                        src_ref=rot.at[1 - core, :, at], dst_ref=rot_in.at[:, at], send_sem=c_sem.at[0, k],
                        recv_sem=c_sem.at[1, k], device_id=partner, device_id_type=MESH,
                    )
                )
                c_copies[k].start()

    lanes, halves = [], []
    for a, b in zip(cuts, cuts[1:]):
        middle = (a + b + 1) // 2
        lanes.append(pl.ds(a * LANES, (b - a) * LANES))
        halves.append((pl.ds(a * LANES, (middle - a) * LANES), pl.ds(middle * LANES, (b - middle) * LANES)))
    ways = ((1, 0), (nz - 1, 1))
    FIRST, MIDDLE, LAST, THROUGH = range(4)

    def z_send(src, dst, sent, landed, k, i):
        return pltpu.make_async_remote_copy(
            src_ref=src, dst_ref=dst, send_sem=z_sem.at[sent, k], recv_sem=z_sem.at[landed, k], device_id=z_peer(i),
            device_id_type=MESH,
        )

    for k, at in enumerate(lanes):
        c_copies[k].wait_recv()

        @pl.loop(0, nz)
        def _(i):
            mine[eight(i), at] = rot[core, eight(i), at] + rot_in[eight(i), at]

        for step, way in ways:
            part = halves[k][way]
            z_send(mine.at[eight(ring(z, nz // 2, nz)), part], z_far.at[way, :, part], FIRST, MIDDLE, k, 2 * step % nz).start()
        for step, way in ways:
            z_send(mine.at[eight(ring(z, 3 * step % nz, nz)), at], z_mid.at[way, :, at], FIRST, MIDDLE, k, step).start()

    for k, at in enumerate(lanes):
        for step, way in ways:
            z_send(mine.at[eight(ring(z, step, nz)), at], z_in.at[way, :, at], FIRST, LAST, k, step).start()

    def through(k):
        at = lanes[k]
        there = z_in.at[pl.ds(0, 3), :, at]
        z_send(there, there, FIRST, MIDDLE, k, 1).wait_recv()
        for step, way in ways:
            z_out[way, :, at] = mine[eight(ring(z, 2 * step % nz, nz)), at] + z_mid[way, :, at]
            z_out[way, :, halves[k][way]] += z_far[way, :, halves[k][way]]
        for step, way in ways:
            z_send(z_out.at[way, :, at], z_in.at[2 + way, :, at], THROUGH, LAST, k, 2 * step % nz).start()

    def transpose(first, last):
        @pl.loop(first, last)
        def _(j):
            at = pl.ds(pl.multiple_of(j * pair, pair), pair)
            to = pl.ds(pl.multiple_of(j * LANES, LANES), LANES)
            for i in range(ny):
                hi, lo = e_hi[i, :, at].T, e_lo[i, :, at].T
                for side in range(2):
                    t_hi[side, i, to, :] = hi[side * LANES:(side + 1) * LANES]
                    t_lo[side, i, to, :] = lo[side * LANES:(side + 1) * LANES]

    all_in(v_all.at[pl.ds(0, nz - 1 - len(close)), corner], V)
    part = v_all.at[:, corner]
    for other in (partner, across, diagonal):
        send(part, part, V2, other).start()

    all_in(g_all.at[pl.ds(0, GROUP * (nt - 1))], G1)
    g_own[...] = g_all[...].T
    g_t[z, xh, own_half] = g_own[own_half, :]

    transpose(0, chunks // 2 + 1)
    for k in range(len(lanes)):
        through(k)
    @pl.loop(1, nz)
    def _(k):
        part = g_t.at[z, xh, own_half]
        send(part, part, G2, z_peer(k)).start()

    transpose(chunks // 2 + 1, chunks - 2)

    def x_copy(k):
        at = lanes[k]
        return pltpu.make_async_remote_copy(
            src_ref=x_out.at[:, at], dst_ref=x_in.at[:, at], send_sem=x_sem.at[0, k], recv_sem=x_sem.at[1, k],
            device_id=across, device_id_type=MESH,
        )

    def ag_send(i, owner, at, k, kind):
        part = s_all.at[core, eight(owner), at]
        return send(part, part, AG, z_peer(i), ag_sem.at[k, kind])

    def fw_send(owner, at, k):
        part = s_all.at[core, eight(owner), at]
        return send(part, part, FW_LAST if k == CHUNKS - 1 else FW, partner)

    for k, at in enumerate(lanes):
        there = z_in.at[:, :, at]
        z_send(there, there, FIRST, LAST, k, 1).wait_recv()
        x_out[:, at] = mine[eight(z), at] + (z_in[0, :, at] + z_in[1, :, at]) + (z_in[2, :, at] + z_in[3, :, at])
        x_copy(k).start()

    all_in(v_all.at[:, pl.ds(0, CORES * XH - 1)], V2)
    for b in range(nrow):
        v_cat[:, b * block:(b + 1) * block] = v_all[b // (CORES * XH), b % (CORES * XH)]
    for j in range(2 * chunks):
        v_use[j % 2, :, (j // 2) * LANES:(j // 2 + 1) * LANES] = v_cat[:, j * LANES:(j + 1) * LANES]

    transpose(chunks - 2, chunks)
    all_out(q_all.at[pl.ds(0, ncol - 1)], Q)
    all_out(g_all.at[pl.ds(0, GROUP * (nt - 1))], G1)
    all_out(v_all.at[pl.ds(0, nz - 1), corner], V)
    all_out(v_all.at[:, pl.ds(0, CORES * XH - 1)], V2)
    for copy in c_copies:
        copy.wait_send()
    for k, at in enumerate(lanes):
        there = mine.at[pl.ds(0, 5 * GROUP), at]
        z_send(there, there, FIRST, LAST, k, 1).wait_send()
        there = z_out.at[:, :, at]
        z_send(there, there, THROUGH, LAST, k, 1).wait_send()
    a_copy.wait()
    hi, lo = split(a_own[...])
    a_hi[...] = hi
    a_lo[...] = lo

    for k, at in enumerate(lanes):
        x_copy(k).wait()
        s_all[core, eight(z), at] = (x_out[:, at] + x_in[:, at]) / (v_use[core, :, at] + damping)
        for step, way in ways:
            ag_send(2 * step % nz, z, at, k, 2 + way).start()
        fw_send(z, at, k).start()

    for k, at in enumerate(lanes):
        for step, way in ways:
            ag_send(step, z, at, k, way).start()

    for k, at in enumerate(lanes):
        for step, way in ways:
            owner = ring(z, nz - 2 * step % nz, nz)
            ag_send(1, owner, at, k, 2 + way).wait_recv()
            ag_send(2 * step % nz, owner, halves[k][way], k, 6 + way).start()
            ag_send(step, owner, at, k, 4 + way).start()
            fw_send(owner, at, k).start()
        if k == 0:
            all_in(g_t.at[pl.ds(0, nz - 1), xh, own_half], G2)
            part = g_t.at[:, xh, own_half]
            send(part, part, G3, across).start()

    early, late = pl.ds(0, cuts[-2] * LANES), lanes[-1]

    def back(side, i, at):
        return folded(
            jnp.dot(s_cat[side, :, at], t_hi[side, i, at, :], preferred_element_type=f32)
            + jnp.dot(s_cat[side, :, at], t_lo[side, i, at, :], preferred_element_type=f32)
        )

    for k, at in enumerate(lanes):
        for away, kind in ((1, 0), (3, 4)):
            for step, way in ways:
                owner = ring(z, nz - away * step % nz, nz)
                ag_send(1, owner, at, k, kind + way).wait_recv()
                fw_send(owner, at, k).start()
        for step, way in ways:
            owner = ring(z, nz // 2, nz)
            ag_send(1, owner, halves[k][way], k, 6 + way).wait_recv()
            fw_send(owner, halves[k][way], k).start()

        if k == CHUNKS - 2:
            s_cat[core, :, early] = stacked(s_all[core, :, early])
            for i in range(ny):
                p_own[i] = back(core, i, early)

    s_cat[core, :, late] = stacked(s_all[core, :, late])
    for i in range(ny):
        p_own[i] += back(core, i, late)
    all_in(g_t.at[:, 1 - xh, own_half], G3)
    part = g_t.at[:, :, own_half]
    send(part, part, G4, partner).start()
    all_in(s_all.at[1 - core, :, early], FW)
    s_cat[1 - core, :, early] = stacked(s_all[1 - core, :, early])
    for i in range(ny):
        p_own[i] += back(1 - core, i, early)
    all_in(s_all.at[1 - core, :, late], FW_LAST)
    s_cat[1 - core, :, late] = stacked(s_all[1 - core, :, late])
    for group in ((3, 2), (1, 0)):
        for i in group:
            part = p_own[i] + back(1 - core, i, late)
            for side in range(XL):
                p_out[i, side] = part[:, side * block:(side + 1) * block]
        for i in group:
            if i == 0:
                send(p_out.at[0, 1 - xl], p_in.at[col], P_, (row, col + 1 - 2 * xl)).start()
            else:
                place = ring(y, near[i], ny)
                for side in range(XL):
                    send(p_out.at[i, side], p_in.at[col], P_, (row, XL * place + side)).start()

    all_in(g_t.at[:, :, pl.ds(pl.multiple_of((1 - core) * (r // CORES), r // CORES), r // CORES)], G4)
    all_out(g_t.at[pl.ds(0, nz - 1), xh, own_half], G2)
    all_out(s_all.at[core, pl.ds(0, GROUP * (nz - 1))], AG)
    all_out(s_all.at[core, :, early], FW)
    all_out(s_all.at[core, :, late], FW_LAST)
    all_out(g_t.at[:, xh, own_half], G3)
    all_out(g_t.at[:, :, own_half], G4)

    all_in(p_in.at[pl.ds(0, ncol - 1)], P_)
    whole = lax.fori_loop(1, ncol, lambda i, total: total + p_in[ring(col, i, ncol)], p_out[0, xl])
    p_ref[...] = whole

    x = stacked(whole)
    for k in range(nchip // 2):
        at = slice(k * pair, (k + 1) * pair)
        projected = folded(
            jnp.dot(x, a_hi[:, at], preferred_element_type=f32) + jnp.dot(x, a_lo[:, at], preferred_element_type=f32)
        )
        for side in range(2):
            there = 2 * k + side
            part = projected[:, side * LANES:(side + 1) * LANES] * g_t[there // XH, there % XH]
            f_out[there // XH, there % XH] = jnp.sum(part, axis=0, keepdims=True)

    place, nplace = CORES * z + core, CORES * nz

    @pl.loop(1, nplace)
    def _(i):
        to = ring(place, i, nplace)
        there = lax.div(to, CORES)
        send(f_out.at[there], f_in.at[place], F1, (CORES * (XH * there + xh) + lax.rem(to, CORES), col)).start()

    all_out(p_in.at[pl.ds(0, ncol - 1)], P_)
    all_in(f_in.at[pl.ds(0, nplace - 1)], F1)
    f_sum[...] = lax.fori_loop(1, nplace, lambda i, total: total + f_in[ring(place, i, nplace)], f_out[z])

    spot, nspot = ncol * xh + col, XH * ncol

    @pl.loop(1, nspot)
    def _(i):
        to = ring(spot, i, nspot)
        there = lax.div(to, ncol)
        send(f_sum.at[there], f_all.at[spot], F2, (CORES * (XH * z + there) + core, lax.rem(to, ncol))).start()

    all_out(f_in.at[pl.ds(0, nplace - 1)], F1)
    all_in(f_all.at[pl.ds(0, nspot - 1)], F2)
    total = lax.fori_loop(1, nspot, lambda i, total: total + f_all[ring(spot, i, nspot)], f_sum[xh])
    total = jnp.broadcast_to(total, (GROUP, LANES))
    s_ref[...] = pltpu.roll(total, lax.rem(LANES - GROUP * t, LANES), axis=1)
    all_out(f_all.at[pl.ds(0, nspot - 1)], F2)


def shards(nrow, ncol, query_slab, eigenbasis, eigenvalues, activations, out_grads):
    depth, width = eigenbasis.shape
    block, r = query_slab.shape
    ntrain = activations.shape[0]
    nchip, nz, ny, nt = nrow // CORES, nrow // (CORES * XH), ncol // XL, CORES * ncol
    wide = pl.cdiv(width, 2 * LANES) * 2 * LANES
    half = wide // 2
    rows = depth // ny
    deep = pl.cdiv(rows, 16) * 16
    v, dma = pltpu.VMEM, pltpu.SemaphoreType.DMA
    anywhere, vmem = pl.BlockSpec(memory_space=pl.ANY), pl.BlockSpec(memory_space=pltpu.VMEM)
    scratch = [
        v((ny, rows, width), f32), v((ny, deep, wide), bf16), v((ny, deep, wide), bf16),
        v((2, ny, half, deep), bf16), v((2, ny, half, deep), bf16),
        v((ncol, r, block), f32), v((r, deep), f32), v((ny, 2 * r, deep), bf16),
        v((2, r, half), f32), v((r, half), f32), v((r, half), f32),
        v((2, GROUP, half), f32), v((2, GROUP, half), f32), v((2, GROUP, half), f32), v((4, GROUP, half), f32),
        v((GROUP, half), f32), v((GROUP, half), f32),
        v((r, block), f32), v((nz, CORES * XH, GROUP, block), f32), v((GROUP, wide), f32), v((2, GROUP, half), f32),
        v((2, r, half), f32), v((2, 2 * r, half), bf16), v((ny, r, deep), f32),
        v((ny, XL, r, block), f32), v((ncol, r, block), f32),
        v((block, ntrain), f32), v((block, ntrain), bf16), v((block, ntrain), bf16),
        v((GROUP * nt, r), f32), v((r, LANES), f32), v((nz, XH, r, LANES), f32),
        v((nz, XH, 1, LANES), f32), v((CORES * nz, XH, 1, LANES), f32), v((XH, 1, LANES), f32), v((nt, 1, LANES), f32),
        dma((ny,)), dma((4,)), dma((2, 13)), dma((4,)), dma((ny,)), dma((2, CHUNKS)), dma((4, CHUNKS)), dma((2, CHUNKS)), dma((CHUNKS, 8)),
    ]
    preconditioned, scores = pl.pallas_call(
        functools.partial(kernel, nrow, ncol),
        out_shape=(pltpu.VMEM((r, block), f32), pltpu.VMEM((GROUP, LANES), f32)),
        in_specs=[anywhere] * 5,
        out_specs=(vmem, vmem),
        scratch_shapes=scratch,
        compiler_params=pltpu.CompilerParams(collective_id=0, has_side_effects=True, vmem_limit_bytes=60 * 2**20),
    )(query_slab.T, eigenbasis, eigenvalues.T, activations.T, out_grads)
    return preconditioned.T, scores[0, :GROUP]


def solution(mesh):
    return jax.shard_map(
        functools.partial(shards, mesh.shape["row"], mesh.shape["col"]),
        mesh=mesh,
        in_specs=(
            P(("row", "col"), None),
            P("row", "col"),
            P(("col", "row"), None),
            P(None, ("row", "col")),
            P(("row", "col"), None),
        ),
        out_specs=(P(("row", "col"), None), P(("row", "col"))),
        check_vma=False,
    )
```

```python
import functools

import jax
import jax.numpy as jnp
from jax import lax
from jax.experimental import pallas as pl
from jax.experimental.pallas import tpu as pltpu
from jax.sharding import PartitionSpec as P

damping = 0.1
MESH = pl.DeviceIdType.MESH
f32, bf16 = jnp.float32, jnp.bfloat16
LANES, GROUP = 128, 8
CHUNKS = 3
CORES = XH = 2
XL = 2


def split(x):
    hi = x.astype(bf16)
    return hi, (x - hi.astype(f32)).astype(bf16)


def stacked(x):
    return jnp.concatenate(split(x), axis=0)


def folded(x):
    half = x.shape[0] // 2
    return x[:half] + x[half:]


def kernel(
    nrow, ncol,
    q_ref, e_ref, v_ref, a_ref, g_ref,
    p_ref, s_ref,
    stage, e_hi, e_lo, t_hi, t_lo, q_all, q_cat, x_cat, rot, rot_in, mine, z_far, z_mid, z_out, z_in, x_out, x_in,
    v_own, v_all, v_cat, v_use, s_all, s_cat, p_own, p_out, p_in,
    a_own, a_hi, a_lo, g_all, g_own, g_t, f_out, f_in, f_sum, f_all,
    e_sem, local, far_sem, one_sem, v_sem, q_sem, c_sem, z_sem, x_sem, ag_sem,
):
    row, col = lax.axis_index("row"), lax.axis_index("col")
    core, chip = lax.rem(row, CORES), lax.div(row, CORES)
    xh, z = lax.rem(chip, XH), lax.div(chip, XH)
    xl, y = lax.rem(col, XL), lax.div(col, XL)
    nchip, nz, ny, nt = nrow // CORES, nrow // (CORES * XH), ncol // XL, CORES * ncol
    t = core * ncol + col
    depth, width = e_ref.shape
    r, block = q_ref.shape
    half = rot.shape[2]
    chunks = half // LANES
    pair = 2 * LANES
    rows = depth // ny
    partner = (row + 1 - 2 * core, col)
    across = (row + 2 - 4 * xh, col)
    near = sorted(range(ny), key=lambda d: min(d, ny - d))
    Q, G1, V, V2, AG, FW, FW_LAST, G2, G3, G4, P_, F1, F2 = range(13)
    corner = XH * xh + core

    def send(src, dst, kind, device, recv=None):
        return pltpu.make_async_remote_copy(
            src_ref=src, dst_ref=dst, send_sem=one_sem.at[0, kind], recv_sem=one_sem.at[1, kind] if recv is None else recv,
            device_id=device, device_id_type=MESH,
        )

    def all_in(ref, kind):
        send(ref, ref, kind, partner).wait_recv()

    def all_out(ref, kind):
        send(ref, ref, kind, partner).wait_send()

    def ring(place, i, n):
        return lax.rem(place + i, n)

    def eight(k):
        return pl.ds(pl.multiple_of(GROUP * k, GROUP), GROUP)

    def e_copy(i):
        at = pl.ds(pl.multiple_of(rows * ring(y, near[i], ny), GROUP), rows)
        return pltpu.make_async_copy(e_ref.at[at], stage.at[i], e_sem.at[i])

    q_copy = pltpu.make_async_copy(q_ref, q_all.at[col], local.at[0])
    g_copy = pltpu.make_async_copy(g_ref, g_all.at[eight(t)], local.at[1])
    v_copy = pltpu.make_async_copy(v_ref, v_own, local.at[2])
    a_copy = pltpu.make_async_copy(a_ref, a_own, local.at[3])
    q_copy.start()
    g_copy.start()
    v_copy.start()
    for i in range(ny):
        e_copy(i).start()
    a_copy.start()

    barrier = pltpu.get_barrier_semaphore()
    diagonal = (across[0] + 1 - 2 * core, col)

    def z_peer(i):
        return (CORES * XH * ring(z, i, nz) + corner, col)

    close = (1, nz - 1, 2, nz - 2)

    beside = [XL * ring(y, d, ny) + side for d in near[1:-1] for side in range(XL)] + [col + 1 - 2 * xl]
    greeted = [(there, other) for other in beside for there in (row, partner[0])]
    greeted += [*(z_peer(i) for i in close), across, diagonal, partner]
    for device in greeted:
        pl.semaphore_signal(barrier, inc=1, device_id=device, device_id_type=MESH)

    def convert(i):
        e_copy(i).wait()

        def put(at, x):
            hi, lo = split(x)
            e_hi[i, at, :width] = hi
            e_lo[i, at, :width] = lo

        @pl.loop(0, rows // 16)
        def _(k):
            at = pl.ds(pl.multiple_of(k * 16, 16), 16)
            put(at, stage[i, at, :])

        done = rows // 16 * 16
        left = jnp.concatenate([stage[i, done:, :], jnp.zeros((e_hi.shape[1] - rows, width), f32)], axis=0)
        put(slice(done, None), left)

    q_copy.wait()
    g_copy.wait()
    v_copy.wait()
    pl.semaphore_wait(barrier, len(greeted))
    pl.semaphore_signal(far_sem, inc=1, device_id=(row, XL * ring(y, 1, ny) + xl), device_id_type=MESH)

    own_q = q_all.at[col]
    send(own_q, own_q, Q, (row, col + 1 - 2 * xl), q_sem.at[0]).start()

    def q_send(places):
        for d in places:
            slot = near.index(ny - d)
            for side in range(XL):
                send(own_q, own_q, Q, (row, XL * ring(y, d, ny) + side), q_sem.at[slot]).start()

    q_send(near[1:-1])

    def v_send(i, owner):
        return send(v_own.at[eight(ring(z, i, nz))], v_all.at[owner, corner], V, z_peer(i))

    def near_v(i, owner):
        return send(v_own.at[eight(ring(z, i, nz))], v_all.at[owner, corner], V, z_peer(i), v_sem.at[close.index(i)])

    for i in close:
        near_v(i, z).start()

    pad = jnp.zeros((e_hi.shape[1], e_hi.shape[2] - width), bf16)
    for i in range(ny):
        e_hi[i, :, width:] = pad
        e_lo[i, :, width:] = pad
    q_cat[:, XL * block:] = jnp.zeros((r, q_cat.shape[1] - XL * block), f32)
    v_cat[:, block * nrow:] = jnp.zeros((GROUP, v_cat.shape[1] - block * nrow), f32)
    v_all[z, corner] = v_own[eight(z), :]
    for i in range(2):
        convert(i)
    pl.semaphore_wait(far_sem, 1)
    q_send(near[-1:])

    @pl.loop(1, nt)
    def _(i):
        to = ring(t, i, nt)
        part = g_all.at[eight(t)]
        send(part, part, G1, (CORES * chip + lax.div(to, ncol), lax.rem(to, ncol))).start()

    for i in range(2, ny):
        convert(i)

    def rotate(i, first, last):
        at = pl.ds(first * pair, (last - first) * pair)
        share = folded(
            jnp.dot(x_cat[i], e_hi[i, :, at], preferred_element_type=f32)
            + jnp.dot(x_cat[i], e_lo[i, :, at], preferred_element_type=f32)
        )
        for j in range(first, last):
            for side in range(2):
                k = 2 * (j - first) + side
                part = share[:, k * LANES:(k + 1) * LANES]
                to = pl.ds(j * LANES, LANES)
                if i == 0:
                    rot[side, :, to] = part
                else:
                    rot[side, :, to] += part

    cuts = [-(-chunks * k // CHUNKS) for k in range(CHUNKS + 1)]
    c_copies = []
    own_half = pl.ds(pl.multiple_of(core * (r // CORES), r // CORES), r // CORES)
    for i in range(ny):
        place = ring(y, near[i], ny)
        if i == 0:
            there = q_all.at[pl.ds(XL * place + 1 - xl, 1)]
        else:
            there = q_all.at[pl.ds(XL * place, XL)]
        send(there, there, Q, partner, q_sem.at[i]).wait_recv()
        for side in range(XL):
            q_cat[:, side * block:(side + 1) * block] = q_all[XL * place + side]
        x_cat[i] = stacked(q_cat[...])
        if i == 0:
            for k in close:
                near_v(k, ring(z, nz - k, nz)).wait_recv()
            for k in range(3, nz - 2):
                v_send(k, z).start()

        for k in range(len(cuts) - 1):
            rotate(i, cuts[k], cuts[k + 1])
            if i == ny - 1:
                at = pl.ds(cuts[k] * LANES, (cuts[k + 1] - cuts[k]) * LANES)
                c_copies.append(
                    pltpu.make_async_remote_copy(
                        src_ref=rot.at[1 - core, :, at], dst_ref=rot_in.at[:, at], send_sem=c_sem.at[0, k],
                        recv_sem=c_sem.at[1, k], device_id=partner, device_id_type=MESH,
                    )
                )
                c_copies[k].start()

    lanes, halves = [], []
    for a, b in zip(cuts, cuts[1:]):
        middle = (a + b + 1) // 2
        lanes.append(pl.ds(a * LANES, (b - a) * LANES))
        halves.append((pl.ds(a * LANES, (middle - a) * LANES), pl.ds(middle * LANES, (b - middle) * LANES)))
    ways = ((1, 0), (nz - 1, 1))
    FIRST, MIDDLE, LAST, THROUGH = range(4)

    def z_send(src, dst, sent, landed, k, i):
        return pltpu.make_async_remote_copy(
            src_ref=src, dst_ref=dst, send_sem=z_sem.at[sent, k], recv_sem=z_sem.at[landed, k], device_id=z_peer(i),
            device_id_type=MESH,
        )

    for k, at in enumerate(lanes):
        c_copies[k].wait_recv()

        @pl.loop(0, nz)
        def _(i):
            mine[eight(i), at] = rot[core, eight(i), at] + rot_in[eight(i), at]

        for step, way in ways:
            part = halves[k][way]
            z_send(mine.at[eight(ring(z, nz // 2, nz)), part], z_far.at[way, :, part], FIRST, MIDDLE, k, 2 * step % nz).start()
        for step, way in ways:
            z_send(mine.at[eight(ring(z, 3 * step % nz, nz)), at], z_mid.at[way, :, at], FIRST, MIDDLE, k, step).start()

    for k, at in enumerate(lanes):
        for step, way in ways:
            z_send(mine.at[eight(ring(z, step, nz)), at], z_in.at[way, :, at], FIRST, LAST, k, step).start()

    def through(k):
        at = lanes[k]
        there = z_in.at[pl.ds(0, 3), :, at]
        z_send(there, there, FIRST, MIDDLE, k, 1).wait_recv()
        for step, way in ways:
            z_out[way, :, at] = mine[eight(ring(z, 2 * step % nz, nz)), at] + z_mid[way, :, at]
            z_out[way, :, halves[k][way]] += z_far[way, :, halves[k][way]]
        for step, way in ways:
            z_send(z_out.at[way, :, at], z_in.at[2 + way, :, at], THROUGH, LAST, k, 2 * step % nz).start()

    def transpose(first, last):
        @pl.loop(first, last)
        def _(j):
            at = pl.ds(pl.multiple_of(j * pair, pair), pair)
            to = pl.ds(pl.multiple_of(j * LANES, LANES), LANES)
            for i in range(ny):
                hi, lo = e_hi[i, :, at].T, e_lo[i, :, at].T
                for side in range(2):
                    t_hi[side, i, to, :] = hi[side * LANES:(side + 1) * LANES]
                    t_lo[side, i, to, :] = lo[side * LANES:(side + 1) * LANES]

    all_in(v_all.at[pl.ds(0, nz - 1 - len(close)), corner], V)
    part = v_all.at[:, corner]
    for other in (partner, across, diagonal):
        send(part, part, V2, other).start()

    all_in(g_all.at[pl.ds(0, GROUP * (nt - 1))], G1)
    g_own[...] = g_all[...].T
    g_t[z, xh, own_half] = g_own[own_half, :]

    transpose(0, chunks // 2 + 1)
    for k in range(len(lanes)):
        through(k)
    @pl.loop(1, nz)
    def _(k):
        part = g_t.at[z, xh, own_half]
        send(part, part, G2, z_peer(k)).start()

    transpose(chunks // 2 + 1, chunks - 2)

    def x_copy(k):
        at = lanes[k]
        return pltpu.make_async_remote_copy(
            src_ref=x_out.at[:, at], dst_ref=x_in.at[:, at], send_sem=x_sem.at[0, k], recv_sem=x_sem.at[1, k],
            device_id=across, device_id_type=MESH,
        )

    def ag_send(i, owner, at, k, kind):
        part = s_all.at[core, eight(owner), at]
        return send(part, part, AG, z_peer(i), ag_sem.at[k, kind])

    def fw_send(owner, at, k):
        part = s_all.at[core, eight(owner), at]
        return send(part, part, FW_LAST if k == CHUNKS - 1 else FW, partner)

    for k, at in enumerate(lanes):
        there = z_in.at[:, :, at]
        z_send(there, there, FIRST, LAST, k, 1).wait_recv()
        x_out[:, at] = mine[eight(z), at] + (z_in[0, :, at] + z_in[1, :, at]) + (z_in[2, :, at] + z_in[3, :, at])
        x_copy(k).start()

    all_in(v_all.at[:, pl.ds(0, CORES * XH - 1)], V2)
    for b in range(nrow):
        v_cat[:, b * block:(b + 1) * block] = v_all[b // (CORES * XH), b % (CORES * XH)]
    for j in range(2 * chunks):
        v_use[j % 2, :, (j // 2) * LANES:(j // 2 + 1) * LANES] = v_cat[:, j * LANES:(j + 1) * LANES]

    transpose(chunks - 2, chunks)
    all_out(q_all.at[pl.ds(0, ncol - 1)], Q)
    all_out(g_all.at[pl.ds(0, GROUP * (nt - 1))], G1)
    all_out(v_all.at[pl.ds(0, nz - 1), corner], V)
    all_out(v_all.at[:, pl.ds(0, CORES * XH - 1)], V2)
    for copy in c_copies:
        copy.wait_send()
    for k, at in enumerate(lanes):
        there = mine.at[pl.ds(0, 5 * GROUP), at]
        z_send(there, there, FIRST, LAST, k, 1).wait_send()
        there = z_out.at[:, :, at]
        z_send(there, there, THROUGH, LAST, k, 1).wait_send()
    a_copy.wait()
    hi, lo = split(a_own[...])
    a_hi[...] = hi
    a_lo[...] = lo

    for k, at in enumerate(lanes):
        x_copy(k).wait()
        s_all[core, eight(z), at] = (x_out[:, at] + x_in[:, at]) / (v_use[core, :, at] + damping)
        for step, way in ways:
            ag_send(2 * step % nz, z, at, k, 2 + way).start()
        fw_send(z, at, k).start()

    for k, at in enumerate(lanes):
        for step, way in ways:
            ag_send(step, z, at, k, way).start()

    for k, at in enumerate(lanes):
        for step, way in ways:
            owner = ring(z, nz - 2 * step % nz, nz)
            ag_send(1, owner, at, k, 2 + way).wait_recv()
            ag_send(2 * step % nz, owner, halves[k][way], k, 6 + way).start()
            ag_send(step, owner, at, k, 4 + way).start()
            fw_send(owner, at, k).start()
        if k == 0:
            all_in(g_t.at[pl.ds(0, nz - 1), xh, own_half], G2)
            part = g_t.at[:, xh, own_half]
            send(part, part, G3, across).start()

    early, late = pl.ds(0, cuts[-2] * LANES), lanes[-1]

    def back(side, i, at):
        return folded(
            jnp.dot(s_cat[side, :, at], t_hi[side, i, at, :], preferred_element_type=f32)
            + jnp.dot(s_cat[side, :, at], t_lo[side, i, at, :], preferred_element_type=f32)
        )

    for k, at in enumerate(lanes):
        for away, kind in ((1, 0), (3, 4)):
            for step, way in ways:
                owner = ring(z, nz - away * step % nz, nz)
                ag_send(1, owner, at, k, kind + way).wait_recv()
                fw_send(owner, at, k).start()
        for step, way in ways:
            owner = ring(z, nz // 2, nz)
            ag_send(1, owner, halves[k][way], k, 6 + way).wait_recv()
            fw_send(owner, halves[k][way], k).start()

        if k == CHUNKS - 2:
            s_cat[core, :, early] = stacked(s_all[core, :, early])
            for i in range(ny):
                p_own[i] = back(core, i, early)

    s_cat[core, :, late] = stacked(s_all[core, :, late])
    for i in range(ny):
        p_own[i] += back(core, i, late)
    all_in(g_t.at[:, 1 - xh, own_half], G3)
    part = g_t.at[:, :, own_half]
    send(part, part, G4, partner).start()
    all_in(s_all.at[1 - core, :, early], FW)
    s_cat[1 - core, :, early] = stacked(s_all[1 - core, :, early])
    for i in range(ny):
        p_own[i] += back(1 - core, i, early)
    all_in(s_all.at[1 - core, :, late], FW_LAST)
    s_cat[1 - core, :, late] = stacked(s_all[1 - core, :, late])
    for group in ((3, 2), (1, 0)):
        for i in group:
            part = p_own[i] + back(1 - core, i, late)
            for side in range(XL):
                p_out[i, side] = part[:, side * block:(side + 1) * block]
        for i in group:
            if i == 0:
                send(p_out.at[0, 1 - xl], p_in.at[col], P_, (row, col + 1 - 2 * xl)).start()
            else:
                place = ring(y, near[i], ny)
                for side in range(XL):
                    send(p_out.at[i, side], p_in.at[col], P_, (row, XL * place + side)).start()

    all_in(g_t.at[:, :, pl.ds(pl.multiple_of((1 - core) * (r // CORES), r // CORES), r // CORES)], G4)
    all_out(g_t.at[pl.ds(0, nz - 1), xh, own_half], G2)
    all_out(s_all.at[core, pl.ds(0, GROUP * (nz - 1))], AG)
    all_out(s_all.at[core, :, early], FW)
    all_out(s_all.at[core, :, late], FW_LAST)
    all_out(g_t.at[:, xh, own_half], G3)
    all_out(g_t.at[:, :, own_half], G4)

    all_in(p_in.at[pl.ds(0, ncol - 1)], P_)
    whole = lax.fori_loop(1, ncol, lambda i, total: total + p_in[ring(col, i, ncol)], p_out[0, xl])
    p_ref[...] = whole

    place, nplace = CORES * z + core, CORES * nz
    x = stacked(whole)
    far = sorted(range(nz), key=lambda i: -min(i, nz - i))
    for group in (far[:nz // 2], far[nz // 2:]):
        for i in group:
            there = ring(z, i, nz)
            at = pl.ds(pl.multiple_of(there * pair, pair), pair)
            projected = folded(
                jnp.dot(x, a_hi[:, at], preferred_element_type=f32)
                + jnp.dot(x, a_lo[:, at], preferred_element_type=f32)
            )
            for side in range(XH):
                part = projected[:, side * LANES:(side + 1) * LANES] * g_t[there, side]
                f_out[there, side] = jnp.sum(part, axis=0, keepdims=True)
        for i in group:
            there = ring(z, i, nz)
            for other in range(CORES) if i else (1 - core,):
                send(f_out.at[there], f_in.at[place], F1, (CORES * (XH * there + xh) + other, col)).start()

    all_out(p_in.at[pl.ds(0, ncol - 1)], P_)
    all_in(f_in.at[pl.ds(0, nplace - 1)], F1)
    f_sum[...] = lax.fori_loop(1, nplace, lambda i, total: total + f_in[ring(place, i, nplace)], f_out[z])

    spot, nspot = ncol * xh + col, XH * ncol

    @pl.loop(1, nspot)
    def _(i):
        to = ring(spot, i, nspot)
        there = lax.div(to, ncol)
        send(f_sum.at[there], f_all.at[spot], F2, (CORES * (XH * z + there) + core, lax.rem(to, ncol))).start()

    all_out(f_in.at[pl.ds(0, nplace - 1)], F1)
    all_in(f_all.at[pl.ds(0, nspot - 1)], F2)
    total = lax.fori_loop(1, nspot, lambda i, total: total + f_all[ring(spot, i, nspot)], f_sum[xh])
    total = jnp.broadcast_to(total, (GROUP, LANES))
    s_ref[...] = pltpu.roll(total, lax.rem(LANES - GROUP * t, LANES), axis=1)
    all_out(f_all.at[pl.ds(0, nspot - 1)], F2)


def shards(nrow, ncol, query_slab, eigenbasis, eigenvalues, activations, out_grads):
    depth, width = eigenbasis.shape
    block, r = query_slab.shape
    ntrain = activations.shape[0]
    nchip, nz, ny, nt = nrow // CORES, nrow // (CORES * XH), ncol // XL, CORES * ncol
    wide = pl.cdiv(width, 2 * LANES) * 2 * LANES
    half = wide // 2
    rows = depth // ny
    deep = pl.cdiv(rows, 16) * 16
    v, dma = pltpu.VMEM, pltpu.SemaphoreType.DMA
    anywhere, vmem = pl.BlockSpec(memory_space=pl.ANY), pl.BlockSpec(memory_space=pltpu.VMEM)
    scratch = [
        v((ny, rows, width), f32), v((ny, deep, wide), bf16), v((ny, deep, wide), bf16),
        v((2, ny, half, deep), bf16), v((2, ny, half, deep), bf16),
        v((ncol, r, block), f32), v((r, deep), f32), v((ny, 2 * r, deep), bf16),
        v((2, r, half), f32), v((r, half), f32), v((r, half), f32),
        v((2, GROUP, half), f32), v((2, GROUP, half), f32), v((2, GROUP, half), f32), v((4, GROUP, half), f32),
        v((GROUP, half), f32), v((GROUP, half), f32),
        v((r, block), f32), v((nz, CORES * XH, GROUP, block), f32), v((GROUP, wide), f32), v((2, GROUP, half), f32),
        v((2, r, half), f32), v((2, 2 * r, half), bf16), v((ny, r, deep), f32),
        v((ny, XL, r, block), f32), v((ncol, r, block), f32),
        v((block, ntrain), f32), v((block, ntrain), bf16), v((block, ntrain), bf16),
        v((GROUP * nt, r), f32), v((r, LANES), f32), v((nz, XH, r, LANES), f32),
        v((nz, XH, 1, LANES), f32), v((CORES * nz, XH, 1, LANES), f32), v((XH, 1, LANES), f32), v((nt, 1, LANES), f32),
        dma((ny,)), dma((4,)), pltpu.SemaphoreType.REGULAR, dma((2, 13)), dma((4,)), dma((ny,)), dma((2, CHUNKS)), dma((4, CHUNKS)), dma((2, CHUNKS)), dma((CHUNKS, 8)),
    ]
    preconditioned, scores = pl.pallas_call(
        functools.partial(kernel, nrow, ncol),
        out_shape=(pltpu.VMEM((r, block), f32), pltpu.VMEM((GROUP, LANES), f32)),
        in_specs=[anywhere] * 5,
        out_specs=(vmem, vmem),
        scratch_shapes=scratch,
        compiler_params=pltpu.CompilerParams(collective_id=0, has_side_effects=True, vmem_limit_bytes=60 * 2**20),
    )(query_slab.T, eigenbasis, eigenvalues.T, activations.T, out_grads)
    return preconditioned.T, scores[0, :GROUP]


def solution(mesh):
    return jax.shard_map(
        functools.partial(shards, mesh.shape["row"], mesh.shape["col"]),
        mesh=mesh,
        in_specs=(
            P(("row", "col"), None),
            P("row", "col"),
            P(("col", "row"), None),
            P(None, ("row", "col")),
            P(("row", "col"), None),
        ),
        out_specs=(P(("row", "col"), None), P(("row", "col"))),
        check_vma=False,
    )
```
